128 devices in a mesh: gx: 8 (over x, core), gy: 16 (over z, y).
Axes of the slice: x: 4, y: 4, z: 4, core: 2. Of those that a mesh axis runs over, the one named last changes fastest.
Arguments:
- phase: float32 [8, 32, 32, 32, 128], P('gx', 'gy'), may hold values from -1 to 1
- solute: float32 [8, 32, 32, 32, 128], P('gx', 'gy'), may hold values from -2.5 to 2.5
- undercool: float32 [8, 32], P('gx', 'gy'), may hold values from -0.5 to 0.5
- mobility: float32 [8, 32], P('gx', 'gy'), may hold values from 0.03 to 0.08
- diffusivity: float32 [8, 32], P('gx', 'gy'), may hold values from 0.04 to 0.14
- owner: int32 [8, 32], P('gx', 'gy'), may hold values from 0 to 127, as said below
Outputs:
- phase_out: float32 [128, 2, 32, 32, 128], P(('gx', 'gy'))
- solute_out: float32 [128, 2, 32, 32, 128], P(('gx', 'gy'))
The draws below stay inside these ranges and needn't reach their ends.
Inputs may be any that keep to these rules, and one draw needn't show every extreme that they name: A tile (p, q) is owned by one of the owners i*16 to i*16+16-1 with i = p. Each owner receives exactly 2 tiles; no device's tiles include more than 1 tiles of one owner, and some device's include exactly 1.
All inputs are finite; a program needn't handle non-finite values.
Results may differ from the reference program's by a relative error of at most 0.0003.
Values sent between devices are 32-bit elements; how exact they have to be, the bound alone decides.
A program may use at most 192 MiB of HBM per device.

```python
import math
import jax
import jax.numpy as jnp

TE = 32
NZ = 128
BX = 1
BY = 2
NSTEPS = 4
TILES_X = 8
TILES_Y = 32
TPD = 2
OWNERS = 128
N_GX = 8
N_GY = 16


def draw_owner(key, part):
    relabel_key, shift_key, tile_key = jax.random.split(key, 3)
    rows_mesh = TILES_X // BX
    cols_mesh = TILES_Y // BY
    tile_perm = jax.random.permutation(tile_key, TPD)
    shift_table = jax.vmap(lambda k: jax.random.permutation(k, cols_mesh))(jax.random.split(shift_key, rows_mesh))
    relabel_table = jax.vmap(lambda k: jax.random.permutation(k, cols_mesh))(jax.random.split(relabel_key, rows_mesh))
    row_index = jnp.arange(TILES_X, dtype=jnp.int32)[:, None]
    col_index = jnp.arange(TILES_Y, dtype=jnp.int32)[None, :]
    mesh_row = row_index // BX + 0 * col_index
    mesh_col = col_index // BY + 0 * row_index
    local_index = row_index % BX * BY + col_index % BY
    within = (shift_table[mesh_row, mesh_col] + tile_perm[local_index]) % cols_mesh
    return (mesh_row * cols_mesh + relabel_table[mesh_row, within]).astype(jnp.int32)


def steps_of(rng, dims, pieces, least, largest):
    factor_of = 1.0
    for position, parts in pieces:
        steps = jax.random.uniform(jax.random.fold_in(jax.random.fold_in(rng, 6), position), (parts,), jnp.float32, least / len(pieces), largest / len(pieces))
        factor_of = factor_of * jnp.repeat(jnp.exp(steps), dims[position] // parts).reshape((-1,) + (1,) * (len(dims) - 1 - position))
    return factor_of


def noise(own_key, extent, deviation, reach, cuts=(), kind=jnp.bfloat16):
    factor_of = steps_of(own_key, extent, cuts, -0.22, 0.18) if cuts else 1.0
    drawn = jax.random.normal(own_key, extent, jnp.float32) * deviation * factor_of
    return jnp.minimum(jnp.maximum(drawn, -reach), reach).astype(kind)


def setup_inputs(seed: int = 0) -> dict:
    seeds = jax.random.split(jax.random.key(seed), 7)
    return {
        "phase": jnp.clip(jax.random.uniform(seeds[0], (TILES_X, TILES_Y, TE, TE, NZ), jnp.float32, -1.0, 1.0) * steps_of(seeds[0], (TILES_X, TILES_Y, TE, TE, NZ), ((0, 8), (1, 16)), -0.4, 0.0), -1.0, 1.0),
        "solute": noise(seeds[1], (TILES_X, TILES_Y, TE, TE, NZ), 0.3, 2.5, ((0, 8), (1, 16)), jnp.float32),
        "undercool": jnp.clip(jax.random.uniform(seeds[2], (TILES_X, TILES_Y), jnp.float32, -0.5, 0.5) * steps_of(seeds[2], (TILES_X, TILES_Y), ((0, 8), (1, 16)), -0.4, 0.0), -0.5, 0.5),
        "mobility": jnp.clip(jnp.exp(math.log(0.08) - 0.98082925 * jax.random.uniform(seeds[3], (TILES_X, TILES_Y), jnp.float32) ** steps_of(seeds[3], (TILES_X, TILES_Y), ((0, 8), (1, 16)), -0.2, 0.2)), 0.03, 0.08),
        "diffusivity": jnp.clip(jnp.exp(math.log(0.14) - 1.252763 * jax.random.uniform(seeds[4], (TILES_X, TILES_Y), jnp.float32) ** steps_of(seeds[4], (TILES_X, TILES_Y), ((0, 8), (1, 16)), -0.2, 0.2)), 0.04, 0.14),
        "owner": draw_owner(jax.random.fold_in(seeds[6], 71), 0),
    }


aniso_strength = 0.05
coupling = 2.0


def step_cells(phase, solute, phase_near, solute_near, under, mobile, spread):
    lower_first, upper_first, lower_second, upper_second, lower_third, upper_third = phase_near
    slope_first = 0.5 * (upper_first - lower_first)
    slope_second = 0.5 * (upper_second - lower_second)
    slope_third = 0.5 * (upper_third - lower_third)
    lap_phase = upper_first + lower_first + upper_second + lower_second + upper_third + lower_third - 6.0 * phase
    sol_lf, sol_uf, sol_ls, sol_us, sol_lt, sol_ut = solute_near
    lap_solute = sol_uf + sol_lf + sol_us + sol_ls + sol_ut + sol_lt - 6.0 * solute
    square_first = slope_first * slope_first
    square_second = slope_second * slope_second
    square_third = slope_third * slope_third
    grad_two = square_first + square_second + square_third
    grad_four = square_first * square_first + square_second * square_second + square_third * square_third
    aniso = 1.0 + aniso_strength * (4.0 * grad_four - 3.0 * grad_two * grad_two) / ((1.0 + grad_two) * (1.0 + grad_two))
    well = 1.0 - phase * phase
    new_phase = phase + mobile * (aniso * lap_phase + phase - phase * phase * phase - coupling * well * well * (under + solute))
    new_solute = solute + spread * lap_solute + 0.5 * (new_phase - phase)
    return new_phase, new_solute


def near_cells(field):
    return (jnp.roll(field, 1, 0), jnp.roll(field, -1, 0), jnp.roll(field, 1, 1), jnp.roll(field, -1, 1),
            jnp.concatenate([field[:, :, :1], field[:, :, :-1]], 2),
            jnp.concatenate([field[:, :, 1:], field[:, :, -1:]], 2))


def assemble(tiles):
    return jnp.transpose(tiles, (0, 2, 1, 3, 4)).reshape(TILES_X * TE, TILES_Y * TE, NZ)


def split_tiles(field):
    return jnp.transpose(field.reshape(TILES_X, TE, TILES_Y, TE, NZ), (0, 2, 1, 3, 4))


def home_order(values):
    rest = values.shape[2:]
    grouped = values.reshape((N_GX, BX, N_GY, BY) + rest)
    grouped = jnp.moveaxis(grouped, 2, 1)
    return grouped.reshape((OWNERS * TPD,) + rest)


def spread_cells(coeff):
    return jnp.repeat(jnp.repeat(coeff, TE, 0), TE, 1)[:, :, None]


def reference(phase, solute, undercool, mobility, diffusivity, owner):
    phase_field = assemble(phase)
    solute_field = assemble(solute)
    under = spread_cells(undercool)
    mobile = spread_cells(mobility)
    spread = spread_cells(diffusivity)
    for iteration in range(NSTEPS):
        phase_field, solute_field = step_cells(phase_field, solute_field, near_cells(phase_field),
                                               near_cells(solute_field), under, mobile, spread)
    owner_flat = home_order(owner)
    ordering = jnp.argsort(owner_flat, stable=True)
    phase_home = home_order(split_tiles(phase_field))[ordering]
    solute_home = home_order(split_tiles(solute_field))[ordering]
    return (phase_home.reshape(OWNERS, TPD, TE, TE, NZ), solute_home.reshape(OWNERS, TPD, TE, TE, NZ))
```

```python
import functools

import jax
import jax.numpy as jnp
from jax import lax
from jax.experimental import pallas as pl
from jax.experimental.pallas import tpu as pltpu
from jax.sharding import PartitionSpec as P

MESH = pl.DeviceIdType.MESH
NSTEPS = 4
RIM = 4
EDGE = 32
DEPTH = 128
GROUPS = 10
CHUNKS = 8
ORDER = (1, 2, 3, 4, 5, 6, 0, 7)

aniso_strength = 0.05
coupling = 2.0


def kernel(
    n_gx, n_gy,
    phase, solute, under_s, mobile_s, spread_s, owner_s,
    out,
    lev, fin, halo, coef, own, ownid, ids, table_v, table_s, stage,
    recv0, recv1, recv2, recv3, recv4, recv5, recv6, recv7,
    in_sem, y_sem, x_sem, c_sem, coef_sem, id_sem, tab_sem, hop1_sem, out_sem,
    halo_send, coef_send, id_send, hop1_send, hop2_send,
):
    recv = (recv0, recv1, recv2, recv3, recv4, recv5, recv6, recv7)
    fields = (phase, solute)
    gx = lax.axis_index("gx")
    gy = lax.axis_index("gy")
    gx_up = lax.rem(gx + 1, n_gx)
    gx_dn = lax.rem(gx + n_gx - 1, n_gx)
    gy_up = lax.rem(gy + 1, n_gy)
    gy_dn = lax.rem(gy + n_gy - 1, n_gy)

    def remote(src, dst, send, recv_sem, device):
        return pltpu.make_async_remote_copy(
            src_ref=src, dst_ref=dst, send_sem=send, recv_sem=recv_sem,
            device_id=device, device_id_type=MESH,
        )

    loads = []
    for f in range(2):
        for b in range(2):
            loads.append(pltpu.make_async_copy(
                fields[f].at[0, b],
                lev.at[0, f, pl.ds(RIM, EDGE), pl.ds(8 + EDGE * b, EDGE), :],
                in_sem.at[2 * f + b],
            ))
    for copy in loads:
        copy.start()

    barrier = pltpu.get_barrier_semaphore()

    @pl.loop(1, n_gy)
    def _(d):
        pl.semaphore_signal(barrier, inc=1, device_id=(gx, lax.rem(gy + d, n_gy)), device_id_type=MESH)

    for device in ((gx_up, gy), (gx_dn, gy), (gx_up, gy_up), (gx_up, gy_dn), (gx_dn, gy_up), (gx_dn, gy_dn)):
        pl.semaphore_signal(barrier, inc=1, device_id=device, device_id_type=MESH)

    for b in range(2):
        for c, values in enumerate((under_s, mobile_s, spread_s)):
            block = jnp.full((8, DEPTH), values[0, b], jnp.float32)
            own[b, c] = block
            coef[1, 1 + b, c] = block
    lane = lax.broadcasted_iota(jnp.int32, (8, DEPTH), 1)
    mine = jnp.where(lane == 2 * gy, owner_s[0, 0], 0) + jnp.where(lane == 2 * gy + 1, owner_s[0, 1], 0)
    ownid[...] = mine

    pl.semaphore_wait(barrier, n_gy + 5)

    halos = []
    for q in range(4):
        for f in range(2):
            rows = pl.ds(8 * q, 8)
            halos.append(remote(
                fields[f].at[0, 1, rows, pl.ds(EDGE - RIM, RIM), :], halo.at[q, f, 0],
                halo_send.at[0], y_sem.at[q], (gx, gy_up)))
            halos.append(remote(
                fields[f].at[0, 0, rows, pl.ds(0, RIM), :], halo.at[q, f, 1],
                halo_send.at[0], y_sem.at[q], (gx, gy_dn)))
        if q == 0:
            smalls = [
                remote(own.at[1], coef.at[1, 0], coef_send.at[0], coef_sem.at[0], (gx, gy_up)),
                remote(own.at[0], coef.at[1, 3], coef_send.at[1], coef_sem.at[1], (gx, gy_dn)),
                remote(own.at[pl.ds(0, 2)], coef.at[0, pl.ds(1, 2)], coef_send.at[2], coef_sem.at[2], (gx_up, gy)),
                remote(own.at[pl.ds(0, 2)], coef.at[2, pl.ds(1, 2)], coef_send.at[3], coef_sem.at[3], (gx_dn, gy)),
                remote(own.at[1], coef.at[0, 0], coef_send.at[4], coef_sem.at[4], (gx_up, gy_up)),
                remote(own.at[0], coef.at[0, 3], coef_send.at[5], coef_sem.at[5], (gx_up, gy_dn)),
                remote(own.at[1], coef.at[2, 0], coef_send.at[6], coef_sem.at[6], (gx_dn, gy_up)),
                remote(own.at[0], coef.at[2, 3], coef_send.at[7], coef_sem.at[7], (gx_dn, gy_dn)),
            ]
            for copy in halos + smalls:
                copy.start()
        else:
            for copy in halos[4 * q:]:
                copy.start()

    faces = []
    for f in range(2):
        for b in range(2):
            rows = pl.ds(8 + EDGE * b, EDGE)
            faces.append(remote(
                fields[f].at[0, b, pl.ds(EDGE - RIM, RIM)], lev.at[0, f, pl.ds(0, RIM), rows, :],
                halo_send.at[1], x_sem.at[0, f, b], (gx_up, gy)))
            faces.append(remote(
                fields[f].at[0, b, pl.ds(0, RIM)], lev.at[0, f, pl.ds(RIM + EDGE, RIM), rows, :],
                halo_send.at[1], x_sem.at[1, f, b], (gx_dn, gy)))
    for f in range(2):
        for xd, (planes, gx_to) in enumerate(((pl.ds(EDGE - RIM, RIM), gx_up), (pl.ds(0, RIM), gx_dn))):
            corner = halo.at[4, f]
            faces.append(remote(
                fields[f].at[0, 1, planes, pl.ds(EDGE - RIM, RIM), :], corner.at[0, pl.ds(RIM * xd, RIM)],
                halo_send.at[2], c_sem, (gx_to, gy_up)))
            faces.append(remote(
                fields[f].at[0, 0, planes, pl.ds(0, RIM), :], corner.at[1, pl.ds(RIM * xd, RIM)],
                halo_send.at[2], c_sem, (gx_to, gy_dn)))
    for copy in faces:
        copy.start()

    def id_copy(d):
        return remote(ownid, ids.at[gy], id_send, id_sem, (gx, lax.rem(gy + d, n_gy)))

    @pl.loop(1, n_gy)
    def _(d):
        id_copy(d).start()

    ids[gy] = mine

    first_lane = lane == 0
    last_lane = lane == DEPTH - 1

    def advance(level, i, q):
        near = []
        for f in range(2):
            low = 8 * q
            mid = lev[level, f, i, pl.ds(low, 8), :]
            lower_x = lev[level, f, i - 1, pl.ds(low, 8), :]
            upper_x = lev[level, f, i + 1, pl.ds(low, 8), :]
            lower_y = pltpu.roll(mid, 1, 0) if q == 0 else lev[level, f, i, pl.ds(low - 1, 8), :]
            upper_y = pltpu.roll(mid, 7, 0) if q == GROUPS - 1 else lev[level, f, i, pl.ds(low + 1, 8), :]
            lower_z = jnp.where(first_lane, mid, pltpu.roll(mid, 1, 1))
            upper_z = jnp.where(last_lane, mid, pltpu.roll(mid, DEPTH - 1, 1))
            near.append((mid, lower_x, upper_x, lower_y, upper_y, lower_z, upper_z))
        zone = (i + EDGE - RIM) // EDGE
        tile = (q + 3) // 4
        under = coef[zone, tile, 0]
        mobile = coef[zone, tile, 1]
        spread = coef[zone, tile, 2]
        p, xl, xu, yl, yu, zl, zu = near[0]
        u, sxl, sxu, syl, syu, szl, szu = near[1]
        dx, dy, dz = xu - xl, yu - yl, zu - zl
        dx2, dy2, dz2 = dx * dx, dy * dy, dz * dz
        two = dx2 + dy2 + dz2
        four = dx2 * dx2 + dy2 * dy2 + dz2 * dz2
        base = two + 4.0
        top = (4.0 * aniso_strength) * four - (3.0 * aniso_strength) * (two * two)
        aniso = 1.0 + top / (base * base)
        lap = (xu + xl) + (yu + yl) + (zu + zl) - 6.0 * p
        lap_u = (sxu + sxl) + (syu + syl) + (szu + szl) - 6.0 * u
        well = 1.0 - p * p
        change = mobile * (aniso * lap + p * well - coupling * (well * well) * (under + u))
        return p + change, u + spread * lap_u + 0.5 * change

    def middle(level, lo, hi):
        @pl.loop(lo, hi)
        def _(i):
            for q in range(GROUPS):
                new_p, new_u = advance(level, i, q)
                lev[level + 1, 0, i, pl.ds(8 * q, 8), :] = new_p
                lev[level + 1, 1, i, pl.ds(8 * q, 8), :] = new_u

    def last(lo, hi):
        @pl.loop(lo, hi)
        def _(i):
            t = (i - RIM) // 2
            h = lax.rem(i - RIM, 2)
            for q in range(1, GROUPS - 1):
                b, g = (q - 1) // 4, (q - 1) % 4
                new_p, new_u = advance(NSTEPS - 1, i, q)
                fin[0, b, t, h, pl.ds(8 * g, 8), :] = new_p
                fin[1, b, t, h, pl.ds(8 * g, 8), :] = new_u

    def spread_rims(lo, n, q, off):
        @pl.loop(0, n)
        def _(i):
            for f in range(2):
                lev[0, f, lo + i, pl.ds(RIM, RIM), :] = halo[q, f, 0, off + i]
                lev[0, f, lo + i, pl.ds(8 + 2 * EDGE, RIM), :] = halo[q, f, 1, off + i]

    def hop1_copy(c, d):
        to = lax.rem(gy + d, n_gy)
        f, g, h = lax.rem(to // 4, 2), lax.rem(to, 4), to // 8
        src = fin.at[f, :, pl.ds(2 * c, 2), h, pl.ds(pl.multiple_of(8 * g, 8), 8), :]
        return src, to

    def hop1(c):
        @pl.loop(1, n_gy)
        def _(d):
            src, to = hop1_copy(c, d)
            remote(src, recv[c].at[pl.ds(2 * gy, 2)], hop1_send.at[c], hop1_sem.at[c], (gx, to)).start()

        src, _ = hop1_copy(c, 0)
        pltpu.make_async_copy(src, recv[c].at[pl.ds(2 * gy, 2)], hop1_sem.at[c]).start()

    my_f, my_g, my_h = lax.rem(gy // 4, 2), lax.rem(gy, 4), gy // 8

    def hop2(c):
        pltpu.make_async_copy(recv[c], recv[c], hop1_sem.at[c]).wait()
        dst = out.at[my_f, :, pl.ds(2 * c, 2), my_h, pl.ds(pl.multiple_of(8 * my_g, 8), 8), :]

        def pick(d):
            to = lax.rem(gy + d, n_gy)
            for j in range(2):
                stage[c, to, j] = recv[c][table_s[j, to, 0]]
            return to

        @pl.loop(1, n_gy)
        def _(d):
            to = pick(d)
            remote(stage.at[c, to], dst, hop2_send.at[c], out_sem, (gx, to)).start()

        to = pick(0)
        pltpu.make_async_copy(stage.at[c, to], dst, out_sem).start()

    for copy in loads:
        copy.wait()
    for k in (0, 1):
        smalls[k].wait_recv()

    done = [5, 6, 7, 8]
    rims = 0
    for c in ORDER[:6]:
        top = 4 * c + 8
        limits = (min(top + 3, 35), min(top + 2, 34), top + 1, top)
        need = min((limits[0] - RIM) // 8 + 1, 4)
        while rims < need:
            pltpu.make_async_copy(halo.at[rims], halo.at[rims], y_sem.at[rims]).wait()
            spread_rims(RIM + 8 * rims, 8, rims, 0)
            rims += 1
        for level in range(NSTEPS - 1):
            middle(level, done[level], limits[level])
        last(done[3], limits[3])
        done = list(limits)
        hop1(c)
        if c == 1:
            others = ids.at[pl.ds(0, n_gy - 1)]
            pltpu.make_async_copy(others, others, id_sem).wait()
            total = ids[0]
            for s in range(1, n_gy):
                total = total + ids[s]
            both = jnp.concatenate([total, total], axis=0)
            lanes = lax.broadcasted_iota(jnp.int32, (n_gy, DEPTH), 1)
            wanted = gx * n_gy + lax.broadcasted_iota(jnp.int32, (n_gy, DEPTH), 0)
            match = (both == wanted) & (lanes < 2 * n_gy)
            least = jnp.min(jnp.where(match, lanes, 2 * n_gy - 1), axis=1, keepdims=True)
            most = jnp.max(jnp.where(match, lanes, 0), axis=1, keepdims=True)
            table_v[0] = jnp.broadcast_to(least, (n_gy, DEPTH))
            table_v[1] = jnp.broadcast_to(most, (n_gy, DEPTH))
            tab = pltpu.make_async_copy(table_v, table_s, tab_sem)
            tab.start()

    for copy in faces[:8]:
        copy.wait_recv()
    for k in range(2, 8):
        smalls[k].wait_recv()
    pltpu.make_async_copy(halo.at[4], halo.at[4], c_sem).wait()
    spread_rims(0, RIM, 4, 0)
    spread_rims(RIM + EDGE, RIM, 4, RIM)
    for level in range(NSTEPS - 1):
        middle(level, 1 + level, 5 + level)
    last(4, 8)
    hop1(0)
    for level in range(NSTEPS - 1):
        middle(level, 35 - level, 39 - level)
    last(32, 36)
    hop1(7)

    tab.wait()
    for c in ORDER:
        hop2(c)

    pltpu.make_async_copy(out, out, out_sem).wait()
    for k, sent in enumerate((halo.at[pl.ds(0, 4)], fin.at[0, 0], halo.at[4])):
        pltpu.make_async_copy(sent, sent, halo_send.at[k]).wait()
    for copy in smalls:
        copy.wait_send()
    others = ids.at[pl.ds(0, n_gy - 1)]
    pltpu.make_async_copy(others, others, id_send).wait()

    for c in range(CHUNKS):
        some = recv[c].at[pl.ds(0, 2 * n_gy - 2)]
        pltpu.make_async_copy(some, some, hop1_send.at[c]).wait()
        pltpu.make_async_copy(some, some, hop2_send.at[c]).wait()


def per_device(n_gx, n_gy, phase, solute, undercool, mobility, diffusivity, owner):
    smem = pl.BlockSpec(memory_space=pltpu.SMEM)
    hbm = pl.BlockSpec(memory_space=pl.ANY)
    f32 = jnp.float32
    dma = pltpu.SemaphoreType.DMA
    out = pl.pallas_call(
        functools.partial(kernel, n_gx, n_gy),
        out_shape=jax.ShapeDtypeStruct((2, 2, 16, 2, EDGE, DEPTH), f32),
        in_specs=[hbm, hbm, smem, smem, smem, smem],
        out_specs=hbm,
        scratch_shapes=[
            pltpu.VMEM((NSTEPS, 2, EDGE + 2 * RIM, 8 * GROUPS, DEPTH), f32),
            pltpu.VMEM((2, 2, 16, 2, EDGE, DEPTH), f32),
            pltpu.VMEM((5, 2, 2, 8, RIM, DEPTH), f32),
            pltpu.VMEM((3, 4, 3, 8, DEPTH), f32),
            pltpu.VMEM((2, 3, 8, DEPTH), f32),
            pltpu.VMEM((8, DEPTH), jnp.int32),
            pltpu.VMEM((n_gy, 8, DEPTH), jnp.int32),
            pltpu.VMEM((2, n_gy, DEPTH), jnp.int32),
            pltpu.SMEM((2, n_gy, DEPTH), jnp.int32),
            pltpu.VMEM((CHUNKS, n_gy, 2, 2, 8, DEPTH), f32),
        ]
        + [pltpu.VMEM((2 * n_gy, 2, 8, DEPTH), f32)] * CHUNKS
        + [
            dma((4,)), dma((4,)), dma((2, 2, 2)), dma(()), dma((8,)), dma(()), dma(()), dma((CHUNKS,)), dma(()),
            dma((3,)), dma((8,)), dma(()), dma((CHUNKS,)), dma((CHUNKS,)),
        ],
        compiler_params=pltpu.CompilerParams(
            collective_id=0, has_side_effects=True, vmem_limit_bytes=56 << 20
        ),
    )(phase, solute, undercool, mobility, diffusivity, owner)
    shape = (1, 2, EDGE, EDGE, DEPTH)
    return out[0].reshape(shape), out[1].reshape(shape)


def solution(mesh):
    in_specs = (
        P("gx", "gy", None, None, None),
        P("gx", "gy", None, None, None),
        P("gx", "gy"),
        P("gx", "gy"),
        P("gx", "gy"),
        P("gx", "gy"),
    )
    out_specs = (P(("gx", "gy"), None, None, None, None), P(("gx", "gy"), None, None, None, None))
    return jax.shard_map(
        functools.partial(per_device, mesh.shape["gx"], mesh.shape["gy"]),
        mesh=mesh, in_specs=in_specs, out_specs=out_specs, check_vma=False,
    )
```

```python
import functools

import jax
import jax.numpy as jnp
from jax import lax
from jax.experimental import pallas as pl
from jax.experimental.pallas import tpu as pltpu
from jax.sharding import PartitionSpec as P

MESH = pl.DeviceIdType.MESH
NSTEPS = 4
RIM = 4
EDGE = 32
DEPTH = 128
GROUPS = 10
CHUNKS = 8
ORDER = (1, 2, 3, 4, 5, 6, 0, 7)

aniso_strength = 0.05
coupling = 2.0


def kernel(
    n_gx, n_gy,
    phase, solute, under_s, mobile_s, spread_s, owner_s,
    out,
    lev, fin, halo, coef, own, ownid, ids, table_v, table_s, stage,
    recv0, recv1, recv2, recv3, recv4, recv5, recv6, recv7,
    in_sem, y_sem, x_sem, c_sem, coef_sem, id_sem, tab_sem, hop1_sem, out_sem,
    halo_send, coef_send, id_send, hop1_send, hop2_send,
):
    recv = (recv0, recv1, recv2, recv3, recv4, recv5, recv6, recv7)
    fields = (phase, solute)
    gx = lax.axis_index("gx")
    gy = lax.axis_index("gy")
    gx_up = lax.rem(gx + 1, n_gx)
    gx_dn = lax.rem(gx + n_gx - 1, n_gx)
    gy_up = lax.rem(gy + 1, n_gy)
    gy_dn = lax.rem(gy + n_gy - 1, n_gy)

    def remote(src, dst, send, recv_sem, device):
        return pltpu.make_async_remote_copy(
            src_ref=src, dst_ref=dst, send_sem=send, recv_sem=recv_sem,
            device_id=device, device_id_type=MESH,
        )

    loads = []
    for f in range(2):
        for b in range(2):
            loads.append(pltpu.make_async_copy(
                fields[f].at[0, b],
                lev.at[0, f, pl.ds(RIM, EDGE), pl.ds(8 + EDGE * b, EDGE), :],
                in_sem.at[2 * f + b],
            ))
    for copy in loads:
        copy.start()

    barrier = pltpu.get_barrier_semaphore()

    @pl.loop(1, n_gy)
    def _(d):
        pl.semaphore_signal(barrier, inc=1, device_id=(gx, lax.rem(gy + d, n_gy)), device_id_type=MESH)

    for device in ((gx_up, gy), (gx_dn, gy), (gx_up, gy_up), (gx_up, gy_dn), (gx_dn, gy_up), (gx_dn, gy_dn)):
        pl.semaphore_signal(barrier, inc=1, device_id=device, device_id_type=MESH)

    for b in range(2):
        for c, values in enumerate((under_s, mobile_s, spread_s)):
            block = jnp.full((8, DEPTH), values[0, b], jnp.float32)
            own[b, c] = block
            coef[1, 1 + b, c] = block
    lane = lax.broadcasted_iota(jnp.int32, (8, DEPTH), 1)
    mine = jnp.where(lane == 2 * gy, owner_s[0, 0], 0) + jnp.where(lane == 2 * gy + 1, owner_s[0, 1], 0)
    ownid[...] = mine

    pl.semaphore_wait(barrier, n_gy + 5)

    halos = []
    for q in range(4):
        for f in range(2):
            rows = pl.ds(8 * q, 8)
            halos.append(remote(
                fields[f].at[0, 1, rows, pl.ds(EDGE - RIM, RIM), :], halo.at[q, f, 0],
                halo_send.at[0], y_sem.at[q], (gx, gy_up)))
            halos.append(remote(
                fields[f].at[0, 0, rows, pl.ds(0, RIM), :], halo.at[q, f, 1],
                halo_send.at[0], y_sem.at[q], (gx, gy_dn)))
        if q == 0:
            smalls = [
                remote(own.at[1], coef.at[1, 0], coef_send.at[0], coef_sem.at[0], (gx, gy_up)),
                remote(own.at[0], coef.at[1, 3], coef_send.at[1], coef_sem.at[1], (gx, gy_dn)),
                remote(own.at[pl.ds(0, 2)], coef.at[0, pl.ds(1, 2)], coef_send.at[2], coef_sem.at[2], (gx_up, gy)),
                remote(own.at[pl.ds(0, 2)], coef.at[2, pl.ds(1, 2)], coef_send.at[3], coef_sem.at[3], (gx_dn, gy)),
                remote(own.at[1], coef.at[0, 0], coef_send.at[4], coef_sem.at[4], (gx_up, gy_up)),
                remote(own.at[0], coef.at[0, 3], coef_send.at[5], coef_sem.at[5], (gx_up, gy_dn)),
                remote(own.at[1], coef.at[2, 0], coef_send.at[6], coef_sem.at[6], (gx_dn, gy_up)),
                remote(own.at[0], coef.at[2, 3], coef_send.at[7], coef_sem.at[7], (gx_dn, gy_dn)),
            ]
            for copy in halos + smalls:
                copy.start()
        else:
            for copy in halos[4 * q:]:
                copy.start()

    faces = []
    for f in range(2):
        for b in range(2):
            rows = pl.ds(8 + EDGE * b, EDGE)
            faces.append(remote(
                fields[f].at[0, b, pl.ds(EDGE - RIM, RIM)], lev.at[0, f, pl.ds(0, RIM), rows, :],
                halo_send.at[1], x_sem.at[0, f, b], (gx_up, gy)))
            faces.append(remote(
                fields[f].at[0, b, pl.ds(0, RIM)], lev.at[0, f, pl.ds(RIM + EDGE, RIM), rows, :],
                halo_send.at[1], x_sem.at[1, f, b], (gx_dn, gy)))
    for f in range(2):
        for xd, (planes, gx_to) in enumerate(((pl.ds(EDGE - RIM, RIM), gx_up), (pl.ds(0, RIM), gx_dn))):
            corner = halo.at[4, f]
            faces.append(remote(
                fields[f].at[0, 1, planes, pl.ds(EDGE - RIM, RIM), :], corner.at[0, pl.ds(RIM * xd, RIM)],
                halo_send.at[2], c_sem, (gx_to, gy_up)))
            faces.append(remote(
                fields[f].at[0, 0, planes, pl.ds(0, RIM), :], corner.at[1, pl.ds(RIM * xd, RIM)],
                halo_send.at[2], c_sem, (gx_to, gy_dn)))
    for copy in faces:
        copy.start()

    def id_copy(d):
        return remote(ownid, ids.at[gy], id_send, id_sem, (gx, lax.rem(gy + d, n_gy)))

    @pl.loop(1, n_gy)
    def _(d):
        id_copy(d).start()

    ids[gy] = mine

    first_lane = lane == 0
    last_lane = lane == DEPTH - 1

    def advance(level, i, q):
        near = []
        for f in range(2):
            low = 8 * q
            mid = lev[level, f, i, pl.ds(low, 8), :]
            lower_x = lev[level, f, i - 1, pl.ds(low, 8), :]
            upper_x = lev[level, f, i + 1, pl.ds(low, 8), :]
            lower_y = pltpu.roll(mid, 1, 0) if q == 0 else lev[level, f, i, pl.ds(low - 1, 8), :]
            upper_y = pltpu.roll(mid, 7, 0) if q == GROUPS - 1 else lev[level, f, i, pl.ds(low + 1, 8), :]
            lower_z = jnp.where(first_lane, mid, pltpu.roll(mid, 1, 1))
            upper_z = jnp.where(last_lane, mid, pltpu.roll(mid, DEPTH - 1, 1))
            near.append((mid, lower_x, upper_x, lower_y, upper_y, lower_z, upper_z))
        zone = (i + EDGE - RIM) // EDGE
        tile = (q + 3) // 4
        under = coef[zone, tile, 0]
        mobile = coef[zone, tile, 1]
        spread = coef[zone, tile, 2]
        p, xl, xu, yl, yu, zl, zu = near[0]
        u, sxl, sxu, syl, syu, szl, szu = near[1]
        dx, dy, dz = xu - xl, yu - yl, zu - zl
        dx2, dy2, dz2 = dx * dx, dy * dy, dz * dz
        two = dx2 + dy2 + dz2
        four = dx2 * dx2 + dy2 * dy2 + dz2 * dz2
        base = two + 4.0
        top = (4.0 * aniso_strength) * four - (3.0 * aniso_strength) * (two * two)
        aniso = 1.0 + top / (base * base)
        lap = (xu + xl) + (yu + yl) + (zu + zl) - 6.0 * p
        lap_u = (sxu + sxl) + (syu + syl) + (szu + szl) - 6.0 * u
        well = 1.0 - p * p
        change = mobile * (aniso * lap + p * well - coupling * (well * well) * (under + u))
        return p + change, u + spread * lap_u + 0.5 * change

    def middle(level, lo, hi):
        @pl.loop(lo, hi)
        def _(i):
            for q in range(GROUPS):
                new_p, new_u = advance(level, i, q)
                lev[level + 1, 0, i, pl.ds(8 * q, 8), :] = new_p
                lev[level + 1, 1, i, pl.ds(8 * q, 8), :] = new_u

    def last(lo, hi):
        @pl.loop(lo, hi)
        def _(i):
            t = (i - RIM) // 2
            h = lax.rem(i - RIM, 2)
            for q in range(1, GROUPS - 1):
                b, g = (q - 1) // 4, (q - 1) % 4
                new_p, new_u = advance(NSTEPS - 1, i, q)
                fin[0, b, t, h, pl.ds(8 * g, 8), :] = new_p
                fin[1, b, t, h, pl.ds(8 * g, 8), :] = new_u

    def spread_rims(lo, n, q, off):
        @pl.loop(0, n)
        def _(i):
            for f in range(2):
                lev[0, f, lo + i, pl.ds(RIM, RIM), :] = halo[q, f, 0, off + i]
                lev[0, f, lo + i, pl.ds(8 + 2 * EDGE, RIM), :] = halo[q, f, 1, off + i]

    def hop1_copy(c, d):
        to = lax.rem(gy + d, n_gy)
        f, g, h = lax.rem(to // 4, 2), lax.rem(to, 4), to // 8
        src = fin.at[f, :, pl.ds(2 * c, 2), h, pl.ds(pl.multiple_of(8 * g, 8), 8), :]
        return src, to

    def hop1(c):
        @pl.loop(1, n_gy)
        def _(d):
            src, to = hop1_copy(c, d)
            remote(src, recv[c].at[pl.ds(2 * gy, 2)], hop1_send.at[c], hop1_sem.at[c], (gx, to)).start()

        src, _ = hop1_copy(c, 0)
        pltpu.make_async_copy(src, recv[c].at[pl.ds(2 * gy, 2)], hop1_sem.at[c]).start()

    my_f, my_g, my_h = lax.rem(gy // 4, 2), lax.rem(gy, 4), gy // 8

    def hop2(c):
        pltpu.make_async_copy(recv[c], recv[c], hop1_sem.at[c]).wait()
        dst = out.at[my_f, :, pl.ds(2 * c, 2), my_h, pl.ds(pl.multiple_of(8 * my_g, 8), 8), :]

        def pick(d):
            to = lax.rem(gy + d, n_gy)
            for j in range(2):
                stage[c, to, j] = recv[c][table_s[j, to, 0]]
            return to

        @pl.loop(1, n_gy)
        def _(d):
            to = pick(d)
            remote(stage.at[c, to], dst, hop2_send.at[c], out_sem, (gx, to)).start()

        to = pick(0)
        pltpu.make_async_copy(stage.at[c, to], dst, out_sem).start()

    for copy in loads:
        copy.wait()
    for k in (0, 1):
        smalls[k].wait_recv()

    done = [5, 6, 7, 8]
    rims = 0
    for c in ORDER[:6]:
        top = 4 * c + 8
        limits = (min(top + 3, 35), min(top + 2, 34), top + 1, top)
        need = min((limits[0] - RIM) // 8 + 1, 4)
        while rims < need:
            pltpu.make_async_copy(halo.at[rims], halo.at[rims], y_sem.at[rims]).wait()
            spread_rims(RIM + 8 * rims, 8, rims, 0)
            rims += 1
        for level in range(NSTEPS - 1):
            middle(level, done[level], limits[level])
        last(done[3], limits[3])
        done = list(limits)
        hop1(c)
        if c == 1:
            others = ids.at[pl.ds(0, n_gy - 1)]
            pltpu.make_async_copy(others, others, id_sem).wait()
            total = ids[0]
            for s in range(1, n_gy):
                total = total + ids[s]
            both = jnp.concatenate([total, total], axis=0)
            lanes = lax.broadcasted_iota(jnp.int32, (n_gy, DEPTH), 1)
            wanted = gx * n_gy + lax.broadcasted_iota(jnp.int32, (n_gy, DEPTH), 0)
            match = (both == wanted) & (lanes < 2 * n_gy)
            least = jnp.min(jnp.where(match, lanes, 2 * n_gy - 1), axis=1, keepdims=True)
            most = jnp.max(jnp.where(match, lanes, 0), axis=1, keepdims=True)
            table_v[0] = jnp.broadcast_to(least, (n_gy, DEPTH))
            table_v[1] = jnp.broadcast_to(most, (n_gy, DEPTH))
            tab = pltpu.make_async_copy(table_v, table_s, tab_sem)
            tab.start()

    for copy in faces[:8]:
        copy.wait_recv()
    for k in range(2, 8):
        smalls[k].wait_recv()
    pltpu.make_async_copy(halo.at[4], halo.at[4], c_sem).wait()
    spread_rims(0, RIM, 4, 0)
    spread_rims(RIM + EDGE, RIM, 4, RIM)
    for level in range(NSTEPS - 1):
        middle(level, 1 + level, 5 + level)
    last(4, 8)
    hop1(0)
    for level in range(NSTEPS - 1):
        middle(level, 35 - level, 39 - level)
    last(32, 36)
    hop1(7)

    tab.wait()
    for c in ORDER:
        hop2(c)

    pltpu.make_async_copy(out, out, out_sem).wait()
    for k, sent in enumerate((halo.at[pl.ds(0, 4)], fin.at[0, 0], halo.at[4])):
        pltpu.make_async_copy(sent, sent, halo_send.at[k]).wait()
    for copy in smalls:
        copy.wait_send()
    others = ids.at[pl.ds(0, n_gy - 1)]
    pltpu.make_async_copy(others, others, id_send).wait()

    for c in range(CHUNKS):
        some = recv[c].at[pl.ds(0, 2 * n_gy - 2)]
        pltpu.make_async_copy(some, some, hop1_send.at[c]).wait()
        pltpu.make_async_copy(some, some, hop2_send.at[c]).wait()


def per_device(n_gx, n_gy, phase, solute, undercool, mobility, diffusivity, owner):
    smem = pl.BlockSpec(memory_space=pltpu.SMEM)
    hbm = pl.BlockSpec(memory_space=pl.ANY)
    f32 = jnp.float32
    dma = pltpu.SemaphoreType.DMA
    out = pl.pallas_call(
        functools.partial(kernel, n_gx, n_gy),
        out_shape=pltpu.VMEM((2, 2, 16, 2, EDGE, DEPTH), f32),
        in_specs=[hbm, hbm, smem, smem, smem, smem],
        out_specs=hbm,
        scratch_shapes=[
            pltpu.VMEM((NSTEPS, 2, EDGE + 2 * RIM, 8 * GROUPS, DEPTH), f32),
            pltpu.VMEM((2, 2, 16, 2, EDGE, DEPTH), f32),
            pltpu.VMEM((5, 2, 2, 8, RIM, DEPTH), f32),
            pltpu.VMEM((3, 4, 3, 8, DEPTH), f32),
            pltpu.VMEM((2, 3, 8, DEPTH), f32),
            pltpu.VMEM((8, DEPTH), jnp.int32),
            pltpu.VMEM((n_gy, 8, DEPTH), jnp.int32),
            pltpu.VMEM((2, n_gy, DEPTH), jnp.int32),
            pltpu.SMEM((2, n_gy, DEPTH), jnp.int32),
            pltpu.VMEM((CHUNKS, n_gy, 2, 2, 8, DEPTH), f32),
        ]
        + [pltpu.VMEM((2 * n_gy, 2, 8, DEPTH), f32)] * CHUNKS
        + [
            dma((4,)), dma((4,)), dma((2, 2, 2)), dma(()), dma((8,)), dma(()), dma(()), dma((CHUNKS,)), dma(()),
            dma((3,)), dma((8,)), dma(()), dma((CHUNKS,)), dma((CHUNKS,)),
        ],
        compiler_params=pltpu.CompilerParams(
            collective_id=0, has_side_effects=True, vmem_limit_bytes=56 << 20
        ),
    )(phase, solute, undercool, mobility, diffusivity, owner)
    shape = (1, 2, EDGE, EDGE, DEPTH)
    return out[0].reshape(shape), out[1].reshape(shape)


def solution(mesh):
    in_specs = (
        P("gx", "gy", None, None, None),
        P("gx", "gy", None, None, None),
        P("gx", "gy"),
        P("gx", "gy"),
        P("gx", "gy"),
        P("gx", "gy"),
    )
    out_specs = (P(("gx", "gy"), None, None, None, None), P(("gx", "gy"), None, None, None, None))
    return jax.shard_map(
        functools.partial(per_device, mesh.shape["gx"], mesh.shape["gy"]),
        mesh=mesh, in_specs=in_specs, out_specs=out_specs, check_vma=False,
    )
```

```python
import functools

import jax
import jax.numpy as jnp
from jax import lax
from jax.experimental import pallas as pl
from jax.experimental.pallas import tpu as pltpu
from jax.sharding import PartitionSpec as P

MESH = pl.DeviceIdType.MESH
NSTEPS = 4
RIM = 4
EDGE = 32
DEPTH = 128
GROUPS = 10
CHUNKS = 8
ORDER = (1, 2, 3, 4, 5, 6, 0, 7)

aniso_strength = 0.05
coupling = 2.0


def kernel(
    n_gx, n_gy,
    phase, solute, under_s, mobile_s, spread_s, owner_s,
    out,
    lev, fin, rim_y, rim_c, coef, own, ownid, ids, table_v, table_s, stage,
    recv0, recv1, recv2, recv3, recv4, recv5, recv6, recv7,
    in_sem, y_sem, x_sem, c_sem, coef_sem, id_sem, tab_sem, hop1_sem, out_sem,
    halo_send, coef_send, id_send, hop1_send, hop2_send,
):
    recv = (recv0, recv1, recv2, recv3, recv4, recv5, recv6, recv7)
    fields = (phase, solute)
    gx = lax.axis_index("gx")
    gy = lax.axis_index("gy")
    gx_up = lax.rem(gx + 1, n_gx)
    gx_dn = lax.rem(gx + n_gx - 1, n_gx)
    gy_up = lax.rem(gy + 1, n_gy)
    gy_dn = lax.rem(gy + n_gy - 1, n_gy)

    def remote(src, dst, send, recv_sem, device):
        return pltpu.make_async_remote_copy(
            src_ref=src, dst_ref=dst, send_sem=send, recv_sem=recv_sem,
            device_id=device, device_id_type=MESH,
        )

    loads = []
    for f in range(2):
        for b in range(2):
            loads.append(pltpu.make_async_copy(
                fields[f].at[0, b],
                lev.at[0, f, pl.ds(RIM, EDGE), pl.ds(8 + EDGE * b, EDGE), :],
                in_sem.at[2 * f + b],
            ))
    for copy in loads:
        copy.start()

    barrier = pltpu.get_barrier_semaphore()

    for d in range(1, 16):
        pl.semaphore_signal(barrier, inc=1, device_id=(gx, lax.rem(gy + d, n_gy)), device_id_type=MESH)

    for device in ((gx_up, gy), (gx_dn, gy), (gx_up, gy_up), (gx_up, gy_dn), (gx_dn, gy_up), (gx_dn, gy_dn)):
        pl.semaphore_signal(barrier, inc=1, device_id=device, device_id_type=MESH)

    for b in range(2):
        for c, values in enumerate((under_s, mobile_s, spread_s)):
            block = jnp.full((8, DEPTH), values[0, b], jnp.float32)
            own[b, c] = block
            coef[1, 1 + b, c] = block
    lane = lax.broadcasted_iota(jnp.int32, (8, DEPTH), 1)
    mine = jnp.where(lane == 2 * gy, owner_s[0, 0], 0) + jnp.where(lane == 2 * gy + 1, owner_s[0, 1], 0)
    ownid[...] = mine

    first_lane = lane == 0
    last_lane = lane == DEPTH - 1

    def advance(level, i, q):
        near = []
        for f in range(2):
            low = 8 * q
            mid = lev[level, f, i, pl.ds(low, 8), :]
            lower_x = lev[level, f, i - 1, pl.ds(low, 8), :]
            upper_x = lev[level, f, i + 1, pl.ds(low, 8), :]
            lower_y = pltpu.roll(mid, 1, 0) if q == 0 else lev[level, f, i, pl.ds(low - 1, 8), :]
            upper_y = pltpu.roll(mid, 7, 0) if q == GROUPS - 1 else lev[level, f, i, pl.ds(low + 1, 8), :]
            lower_z = jnp.where(first_lane, mid, pltpu.roll(mid, 1, 1))
            upper_z = jnp.where(last_lane, mid, pltpu.roll(mid, DEPTH - 1, 1))
            near.append((mid, lower_x, upper_x, lower_y, upper_y, lower_z, upper_z))
        zone = (i + EDGE - RIM) // EDGE
        tile = (q + 3) // 4
        under = coef[zone, tile, 0]
        mobile = coef[zone, tile, 1]
        spread = coef[zone, tile, 2]
        p, xl, xu, yl, yu, zl, zu = near[0]
        u, sxl, sxu, syl, syu, szl, szu = near[1]
        dx, dy, dz = xu - xl, yu - yl, zu - zl
        dx2, dy2, dz2 = dx * dx, dy * dy, dz * dz
        two = dx2 + dy2 + dz2
        four = dx2 * dx2 + dy2 * dy2 + dz2 * dz2
        base = two + 4.0
        top = (4.0 * aniso_strength) * four - (3.0 * aniso_strength) * (two * two)
        aniso = 1.0 + top / (base * base)
        lap = (xu + xl) + (yu + yl) + (zu + zl) - 6.0 * p
        lap_u = (sxu + sxl) + (syu + syl) + (szu + szl) - 6.0 * u
        well = 1.0 - p * p
        change = mobile * (aniso * lap + p * well - coupling * (well * well) * (under + u))
        return p + change, u + spread * lap_u + 0.5 * change

    def sweep(first, groups, last_groups, starts, pairs):
        @pl.loop(0, NSTEPS - 1)
        def _(level):
            @pl.loop(0, pairs(level))
            def _(n):
                for m in range(2):
                    i = starts(level) + 2 * n + m
                    for q in groups:
                        new_p, new_u = advance(level, i, q)
                        lev[level + 1, 0, i, pl.ds(8 * q, 8), :] = new_p
                        lev[level + 1, 1, i, pl.ds(8 * q, 8), :] = new_u

        @pl.loop(0, 2)
        def _(n):
            for m in range(2):
                i = first + RIM + 2 * n + m
                for q in last_groups:
                    b, g = (q - 1) // 4, (q - 1) % 4
                    new_p, new_u = advance(NSTEPS - 1, i, q)
                    fin[0, b, first // 2 + n, m, pl.ds(8 * g, 8), :] = new_p
                    fin[1, b, first // 2 + n, m, pl.ds(8 * g, 8), :] = new_u

    def sweep_inner(c, groups, last_groups):
        if c == 1:
            sweep(4, groups, last_groups, lambda level: 5 + level, lambda level: 5 - level)
        else:
            sweep(4 * c, groups, last_groups, lambda level: 4 * c + 7 - level, lambda level: 2)

    z, y = gy // 4, lax.rem(gy, 4)
    parity = lax.rem(z + y, 2)
    half = y // 2

    def piece(to_z, to_y, odd):
        side = to_y // 2
        g = 3 * side if odd else 1 + side
        return lax.rem(to_z, 2), pl.multiple_of(8 * g, 8), to_z // 2

    def hop1(c, odd):
        for dz in range(4):
            to_z = lax.rem(z + dz, 4)
            for m in range(2):
                to_y = 2 * lax.rem(half + m, 2) + lax.rem(to_z + odd + c, 2)
                f, row, h = piece(to_z, to_y, odd)
                src = fin.at[f, :, pl.ds(2 * c, 2), h, pl.ds(row, 8), :]
                dst = recv[c].at[pl.ds(2 * gy, 2)]

                def away():
                    remote(src, dst, hop1_send.at[c], hop1_sem.at[c], (gx, 4 * to_z + to_y)).start()

                if dz == 0 and m == 0:
                    pl.when(parity != (odd + c) % 2)(away)

                    @pl.when(parity == (odd + c) % 2)
                    def _():
                        pltpu.make_async_copy(src, dst, hop1_sem.at[c]).start()
                else:
                    away()

    my_f, my_h = lax.rem(z, 2), z // 2

    def hop2(c):
        pltpu.make_async_copy(recv[c], recv[c], hop1_sem.at[c]).wait()
        odd = lax.rem(parity + c, 2)
        row = pl.multiple_of(8 * ((1 - odd) * (1 + half) + odd * 3 * half), 8)
        dst = out.at[my_f, :, pl.ds(2 * c, 2), my_h, pl.ds(row, 8), :]
        for dz in range(4):
            for dy in range(4):
                to = 4 * lax.rem(z + dz, 4) + lax.rem(y + dy, 4)
                for j in range(2):
                    stage[c, to, j] = recv[c][table_s[j, to, 0]]
                if dz or dy:
                    remote(stage.at[c, to], dst, hop2_send.at[c], out_sem, (gx, to)).start()
                else:
                    pltpu.make_async_copy(stage.at[c, to], dst, out_sem).start()

    for copy in loads:
        copy.wait()
    inner, inner_last = range(1, GROUPS - 1), range(2, GROUPS - 2)
    sweep_inner(1, inner, inner_last)

    pl.semaphore_wait(barrier, n_gy + 5)

    for f in range(2):
        remote(fields[f].at[0, 1, :, pl.ds(EDGE - RIM, RIM), :], rim_y.at[f, 0], halo_send.at[0], y_sem, (gx, gy_up)).start()
        remote(fields[f].at[0, 0, :, pl.ds(0, RIM), :], rim_y.at[f, 1], halo_send.at[0], y_sem, (gx, gy_dn)).start()
    smalls = [
        remote(own.at[1], coef.at[1, 0], coef_send.at[0], coef_sem.at[0], (gx, gy_up)),
        remote(own.at[0], coef.at[1, 3], coef_send.at[1], coef_sem.at[1], (gx, gy_dn)),
        remote(own.at[pl.ds(0, 2)], coef.at[0, pl.ds(1, 2)], coef_send.at[2], coef_sem.at[2], (gx_up, gy)),
        remote(own.at[pl.ds(0, 2)], coef.at[2, pl.ds(1, 2)], coef_send.at[3], coef_sem.at[3], (gx_dn, gy)),
        remote(own.at[1], coef.at[0, 0], coef_send.at[4], coef_sem.at[4], (gx_up, gy_up)),
        remote(own.at[0], coef.at[0, 3], coef_send.at[5], coef_sem.at[5], (gx_up, gy_dn)),
        remote(own.at[1], coef.at[2, 0], coef_send.at[6], coef_sem.at[6], (gx_dn, gy_up)),
        remote(own.at[0], coef.at[2, 3], coef_send.at[7], coef_sem.at[7], (gx_dn, gy_dn)),
    ]
    for copy in smalls[:2]:
        copy.start()
    hop1(1, 0)

    faces = []
    for f in range(2):
        for b in range(2):
            rows = pl.ds(8 + EDGE * b, EDGE)
            faces.append(remote(
                fields[f].at[0, b, pl.ds(EDGE - RIM, RIM)], lev.at[0, f, pl.ds(0, RIM), rows, :],
                halo_send.at[1], x_sem.at[0, f, b], (gx_up, gy)))
            faces.append(remote(
                fields[f].at[0, b, pl.ds(0, RIM)], lev.at[0, f, pl.ds(RIM + EDGE, RIM), rows, :],
                halo_send.at[1], x_sem.at[1, f, b], (gx_dn, gy)))
    corners = []
    for f in range(2):
        for xd, (planes, gx_to) in enumerate(((pl.ds(EDGE - RIM, RIM), gx_up), (pl.ds(0, RIM), gx_dn))):
            corners.append(remote(
                fields[f].at[0, 1, planes, pl.ds(EDGE - RIM, RIM), :], rim_c.at[f, 0, pl.ds(RIM * xd, RIM)],
                halo_send.at[2], c_sem, (gx_to, gy_up)))
            corners.append(remote(
                fields[f].at[0, 0, planes, pl.ds(0, RIM), :], rim_c.at[f, 1, pl.ds(RIM * xd, RIM)],
                halo_send.at[2], c_sem, (gx_to, gy_dn)))
    for copy in faces + corners + smalls[2:]:
        copy.start()

    for d in range(1, 16):
        remote(ownid, ids.at[gy], id_send, id_sem, (gx, lax.rem(gy + d, n_gy))).start()
    ids[gy] = mine

    for c in range(2, 7):
        sweep_inner(c, inner, inner_last)
        hop1(c, 0)

    pltpu.make_async_copy(rim_y, rim_y, y_sem).wait()
    for copy in smalls[:2]:
        copy.wait_recv()

    def rims(source, lo, n, off):
        @pl.loop(0, n)
        def _(i):
            for f in range(2):
                lev[0, f, lo + i, pl.ds(RIM, RIM), :] = source[f, 0, off + i]
                lev[0, f, lo + i, pl.ds(8 + 2 * EDGE, RIM), :] = source[f, 1, off + i]

    rims(rim_y, RIM, EDGE, 0)
    for c in range(1, 7):
        sweep_inner(c, (0, 1, GROUPS - 2, GROUPS - 1), (1, GROUPS - 2))
        hop1(c, 1)

    others = ids.at[pl.ds(0, n_gy - 1)]
    pltpu.make_async_copy(others, others, id_sem).wait()
    total = ids[0]
    for s in range(1, 16):
        total = total + ids[s]
    both = jnp.concatenate([total, total], axis=0)
    lanes = lax.broadcasted_iota(jnp.int32, (n_gy, DEPTH), 1)
    wanted = gx * n_gy + lax.broadcasted_iota(jnp.int32, (n_gy, DEPTH), 0)
    match = (both == wanted) & (lanes < 2 * n_gy)
    least = jnp.min(jnp.where(match, lanes, 2 * n_gy - 1), axis=1, keepdims=True)
    most = jnp.max(jnp.where(match, lanes, 0), axis=1, keepdims=True)
    table_v[0] = jnp.broadcast_to(least, (n_gy, DEPTH))
    table_v[1] = jnp.broadcast_to(most, (n_gy, DEPTH))
    tab = pltpu.make_async_copy(table_v, table_s, tab_sem)
    tab.start()

    for copy in faces:
        copy.wait_recv()
    for copy in smalls[2:]:
        copy.wait_recv()
    pltpu.make_async_copy(rim_c, rim_c, c_sem).wait()
    rims(rim_c, 0, RIM, 0)
    rims(rim_c, RIM + EDGE, RIM, RIM)
    every, every_last = range(GROUPS), range(1, GROUPS - 1)
    for c, starts in ((0, lambda level: 1 + level), (7, lambda level: 35 - level)):
        sweep(4 * c, every, every_last, starts, lambda level: 2)
        hop1(c, 0)
        hop1(c, 1)

    tab.wait()
    for c in ORDER:
        hop2(c)

    pltpu.make_async_copy(out, out, out_sem).wait()
    for k, sent in enumerate((rim_y, fin.at[0, 0], rim_c)):
        pltpu.make_async_copy(sent, sent, halo_send.at[k]).wait()
    for copy in smalls:
        copy.wait_send()
    pltpu.make_async_copy(others, others, id_send).wait()
    for c in range(CHUNKS):
        some = recv[c].at[pl.ds(0, 2 * n_gy - 2)]
        pltpu.make_async_copy(some, some, hop1_send.at[c]).wait()
        pltpu.make_async_copy(some, some, hop2_send.at[c]).wait()


def per_device(n_gx, n_gy, phase, solute, undercool, mobility, diffusivity, owner):
    smem = pl.BlockSpec(memory_space=pltpu.SMEM)
    hbm = pl.BlockSpec(memory_space=pl.ANY)
    f32 = jnp.float32
    dma = pltpu.SemaphoreType.DMA
    out = pl.pallas_call(
        functools.partial(kernel, n_gx, n_gy),
        out_shape=pltpu.VMEM((2, 2, 16, 2, EDGE, DEPTH), f32),
        in_specs=[hbm, hbm, smem, smem, smem, smem],
        out_specs=hbm,
        scratch_shapes=[
            pltpu.VMEM((NSTEPS, 2, EDGE + 2 * RIM, 8 * GROUPS, DEPTH), f32),
            pltpu.VMEM((2, 2, 16, 2, EDGE, DEPTH), f32),
            pltpu.VMEM((2, 2, EDGE, RIM, DEPTH), f32),
            pltpu.VMEM((2, 2, 2 * RIM, RIM, DEPTH), f32),
            pltpu.VMEM((3, 4, 3, 8, DEPTH), f32),
            pltpu.VMEM((2, 3, 8, DEPTH), f32),
            pltpu.VMEM((8, DEPTH), jnp.int32),
            pltpu.VMEM((n_gy, 8, DEPTH), jnp.int32),
            pltpu.VMEM((2, n_gy, DEPTH), jnp.int32),
            pltpu.SMEM((2, n_gy, DEPTH), jnp.int32),
            pltpu.VMEM((CHUNKS, n_gy, 2, 2, 8, DEPTH), f32),
        ]
        + [pltpu.VMEM((2 * n_gy, 2, 8, DEPTH), f32)] * CHUNKS
        + [
            dma((4,)), dma(()), dma((2, 2, 2)), dma(()), dma((8,)), dma(()), dma(()), dma((CHUNKS,)), dma(()),
            dma((3,)), dma((8,)), dma(()), dma((CHUNKS,)), dma((CHUNKS,)),
        ],
        compiler_params=pltpu.CompilerParams(
            collective_id=0, has_side_effects=True, vmem_limit_bytes=56 << 20
        ),
    )(phase, solute, undercool, mobility, diffusivity, owner)
    shape = (1, 2, EDGE, EDGE, DEPTH)
    return out[0].reshape(shape), out[1].reshape(shape)


def solution(mesh):
    in_specs = (
        P("gx", "gy", None, None, None),
        P("gx", "gy", None, None, None),
        P("gx", "gy"),
        P("gx", "gy"),
        P("gx", "gy"),
        P("gx", "gy"),
    )
    out_specs = (P(("gx", "gy"), None, None, None, None), P(("gx", "gy"), None, None, None, None))
    return jax.shard_map(
        functools.partial(per_device, mesh.shape["gx"], mesh.shape["gy"]),
        mesh=mesh, in_specs=in_specs, out_specs=out_specs, check_vma=False,
    )
```

```python
import functools

import jax
import jax.numpy as jnp
from jax import lax
from jax.experimental import pallas as pl
from jax.experimental.pallas import tpu as pltpu
from jax.sharding import PartitionSpec as P

MESH = pl.DeviceIdType.MESH
NSTEPS = 4
RIM = 4
EDGE = 32
DEPTH = 128
GROUPS = 10
CHUNKS = 8
ORDER = (1, 2, 3, 4, 5, 6, 0, 7)

aniso_strength = 0.05
coupling = 2.0


def kernel(
    n_gx, n_gy,
    phase, solute, under_s, mobile_s, spread_s, owner_s,
    out,
    lev, fin, rim_y, rim_c, coef, packs, own, ownid, ids, table_v, table_s, stage,
    recv0, recv1, recv2, recv3, recv4, recv5, recv6, recv7,
    in_sem, y_sem, x_sem, c_sem, coef_sem, id_sem, tab_sem, hop1_sem, out_sem,
    halo_send, coef_send, id_send, hop1_send, hop2_send,
):
    recv = (recv0, recv1, recv2, recv3, recv4, recv5, recv6, recv7)
    fields = (phase, solute)
    gx = lax.axis_index("gx")
    gy = lax.axis_index("gy")
    gx_up = lax.rem(gx + 1, n_gx)
    gx_dn = lax.rem(gx + n_gx - 1, n_gx)
    gy_up = lax.rem(gy + 1, n_gy)
    gy_dn = lax.rem(gy + n_gy - 1, n_gy)

    def remote(src, dst, send, recv_sem, device):
        return pltpu.make_async_remote_copy(
            src_ref=src, dst_ref=dst, send_sem=send, recv_sem=recv_sem,
            device_id=device, device_id_type=MESH,
        )

    loads = []
    for f in range(2):
        for b in range(2):
            loads.append(pltpu.make_async_copy(
                fields[f].at[0, b],
                lev.at[0, f, pl.ds(RIM, EDGE), pl.ds(8 + EDGE * b, EDGE), :],
                in_sem.at[2 * f + b],
            ))
    for copy in loads:
        copy.start()

    barrier = pltpu.get_barrier_semaphore()

    for d in range(1, 16):
        pl.semaphore_signal(barrier, inc=1, device_id=(gx, lax.rem(gy + d, n_gy)), device_id_type=MESH)

    for device in ((gx_up, gy), (gx_dn, gy), (gx_up, gy_up), (gx_up, gy_dn), (gx_dn, gy_up), (gx_dn, gy_dn)):
        pl.semaphore_signal(barrier, inc=1, device_id=device, device_id_type=MESH)

    line = lax.broadcasted_iota(jnp.int32, (8, DEPTH), 0)
    for b in range(2):
        packed = jnp.zeros((8, DEPTH), jnp.float32)
        for c, values in enumerate((under_s, mobile_s, spread_s)):
            block = jnp.full((8, DEPTH), values[0, b], jnp.float32)
            packed = jnp.where(line == c, block, packed)
            coef[1, 1 + b, c] = block
        own[b] = packed
    lane = lax.broadcasted_iota(jnp.int32, (8, DEPTH), 1)
    mine = jnp.where(lane == 2 * gy, owner_s[0, 0], 0) + jnp.where(lane == 2 * gy + 1, owner_s[0, 1], 0)
    ownid[...] = mine[:1]

    first_lane = lane == 0
    last_lane = lane == DEPTH - 1

    def advance(level, i, q):
        near = []
        for f in range(2):
            low = 8 * q
            mid = lev[level, f, i, pl.ds(low, 8), :]
            lower_x = lev[level, f, i - 1, pl.ds(low, 8), :]
            upper_x = lev[level, f, i + 1, pl.ds(low, 8), :]
            lower_y = pltpu.roll(mid, 1, 0) if q == 0 else lev[level, f, i, pl.ds(low - 1, 8), :]
            upper_y = pltpu.roll(mid, 7, 0) if q == GROUPS - 1 else lev[level, f, i, pl.ds(low + 1, 8), :]
            lower_z = jnp.where(first_lane, mid, pltpu.roll(mid, 1, 1))
            upper_z = jnp.where(last_lane, mid, pltpu.roll(mid, DEPTH - 1, 1))
            near.append((mid, lower_x, upper_x, lower_y, upper_y, lower_z, upper_z))
        zone = (i + EDGE - RIM) // EDGE
        tile = (q + 3) // 4
        under = coef[zone, tile, 0]
        mobile = coef[zone, tile, 1]
        spread = coef[zone, tile, 2]
        p, xl, xu, yl, yu, zl, zu = near[0]
        u, sxl, sxu, syl, syu, szl, szu = near[1]
        dx, dy, dz = xu - xl, yu - yl, zu - zl
        dx2, dy2, dz2 = dx * dx, dy * dy, dz * dz
        two = dx2 + dy2 + dz2
        four = dx2 * dx2 + dy2 * dy2 + dz2 * dz2
        base = two + 4.0
        top = (4.0 * aniso_strength) * four - (3.0 * aniso_strength) * (two * two)
        aniso = 1.0 + top / (base * base)
        lap = (xu + xl) + (yu + yl) + (zu + zl) - 6.0 * p
        lap_u = (sxu + sxl) + (syu + syl) + (szu + szl) - 6.0 * u
        well = 1.0 - p * p
        change = mobile * (aniso * lap + p * well - coupling * (well * well) * (under + u))
        return p + change, u + spread * lap_u + 0.5 * change

    def sweep(first, groups, last_groups, starts, pairs):
        @pl.loop(0, NSTEPS - 1)
        def _(level):
            @pl.loop(0, pairs(level))
            def _(n):
                for m in range(2):
                    i = starts(level) + 2 * n + m
                    for q in groups:
                        new_p, new_u = advance(level, i, q)
                        lev[level + 1, 0, i, pl.ds(8 * q, 8), :] = new_p
                        lev[level + 1, 1, i, pl.ds(8 * q, 8), :] = new_u

        @pl.loop(0, 2)
        def _(n):
            for m in range(2):
                i = first + RIM + 2 * n + m
                for q in last_groups:
                    b, g = (q - 1) // 4, (q - 1) % 4
                    new_p, new_u = advance(NSTEPS - 1, i, q)
                    fin[0, b, first // 2 + n, m, pl.ds(8 * g, 8), :] = new_p
                    fin[1, b, first // 2 + n, m, pl.ds(8 * g, 8), :] = new_u

    def sweep_inner(c, groups, last_groups):
        opening = 1 - (c + 3) // 5
        sweep(
            4 * c, groups, last_groups,
            lambda level: 4 * c + 7 - level - opening * (6 - 2 * level), lambda level: 2 + opening * (3 - level),
        )

    z, y = gy // 4, lax.rem(gy, 4)
    parity = lax.rem(z + y, 2)
    half = y // 2

    def piece(to_z, to_y, odd):
        side = to_y // 2
        g = 3 * side if odd else 1 + side
        return lax.rem(to_z, 2), pl.multiple_of(8 * g, 8), to_z // 2

    def hop1(c, odd):
        for dz in range(4):
            to_z = lax.rem(z + dz, 4)
            for m in range(2):
                to_y = 2 * lax.rem(half + m, 2) + lax.rem(to_z + odd + c, 2)
                f, row, h = piece(to_z, to_y, odd)
                src = fin.at[f, :, pl.ds(2 * c, 2), h, pl.ds(row, 8), :]
                dst = recv[c].at[pl.ds(2 * gy, 2)]

                def away():
                    remote(src, dst, hop1_send.at[c], hop1_sem.at[c], (gx, 4 * to_z + to_y)).start()

                if dz == 0 and m == 0:
                    pl.when(parity != (odd + c) % 2)(away)

                    @pl.when(parity == (odd + c) % 2)
                    def _():
                        pltpu.make_async_copy(src, dst, hop1_sem.at[c]).start()
                else:
                    away()

    my_f, my_h = lax.rem(z, 2), z // 2

    def hop2(c):
        pltpu.make_async_copy(recv[c], recv[c], hop1_sem.at[c]).wait()
        odd = lax.rem(parity + c, 2)
        row = pl.multiple_of(8 * ((1 - odd) * (1 + half) + odd * 3 * half), 8)
        dst = out.at[my_f, :, pl.ds(2 * c, 2), my_h, pl.ds(row, 8), :]
        for dz in range(4):
            for dy in range(4):
                to = 4 * lax.rem(z + dz, 4) + lax.rem(y + dy, 4)
                for j in range(2):
                    stage[c, to, j] = recv[c][table_s[j, to, 0]]
                if dz or dy:
                    remote(stage.at[c, to], dst, hop2_send.at[c], out_sem, (gx, to)).start()
                else:
                    pltpu.make_async_copy(stage.at[c, to], dst, out_sem).start()

    pl.semaphore_wait(barrier, n_gy + 5)

    for f in range(2):
        remote(fields[f].at[0, 1, :, pl.ds(EDGE - RIM, RIM), :], rim_y.at[f, 0], halo_send.at[0], y_sem, (gx, gy_up)).start()
        remote(fields[f].at[0, 0, :, pl.ds(0, RIM), :], rim_y.at[f, 1], halo_send.at[0], y_sem, (gx, gy_dn)).start()
    smalls = [
        remote(own.at[1], packs.at[1, 0], coef_send.at[0], coef_sem.at[0], (gx, gy_up)),
        remote(own.at[0], packs.at[1, 3], coef_send.at[1], coef_sem.at[1], (gx, gy_dn)),
        remote(own.at[pl.ds(0, 2)], packs.at[0, pl.ds(1, 2)], coef_send.at[2], coef_sem.at[2], (gx_up, gy)),
        remote(own.at[pl.ds(0, 2)], packs.at[2, pl.ds(1, 2)], coef_send.at[3], coef_sem.at[3], (gx_dn, gy)),
        remote(own.at[1], packs.at[0, 0], coef_send.at[4], coef_sem.at[4], (gx_up, gy_up)),
        remote(own.at[0], packs.at[0, 3], coef_send.at[5], coef_sem.at[5], (gx_up, gy_dn)),
        remote(own.at[1], packs.at[2, 0], coef_send.at[6], coef_sem.at[6], (gx_dn, gy_up)),
        remote(own.at[0], packs.at[2, 3], coef_send.at[7], coef_sem.at[7], (gx_dn, gy_dn)),
    ]
    for copy in smalls[:2]:
        copy.start()
    for copy in loads:
        copy.wait()
    faces = []
    for f in range(2):
        for b in range(2):
            rows = pl.ds(8 + EDGE * b, EDGE)
            faces.append(remote(
                fields[f].at[0, b, pl.ds(EDGE - RIM, RIM)], lev.at[0, f, pl.ds(0, RIM), rows, :],
                halo_send.at[1], x_sem.at[0, f, b], (gx_up, gy)))
            faces.append(remote(
                fields[f].at[0, b, pl.ds(0, RIM)], lev.at[0, f, pl.ds(RIM + EDGE, RIM), rows, :],
                halo_send.at[1], x_sem.at[1, f, b], (gx_dn, gy)))
    corners = []
    for f in range(2):
        for xd, (planes, gx_to) in enumerate(((pl.ds(EDGE - RIM, RIM), gx_up), (pl.ds(0, RIM), gx_dn))):
            corners.append(remote(
                fields[f].at[0, 1, planes, pl.ds(EDGE - RIM, RIM), :], rim_c.at[f, 0, pl.ds(RIM * xd, RIM)],
                halo_send.at[2], c_sem, (gx_to, gy_up)))
            corners.append(remote(
                fields[f].at[0, 0, planes, pl.ds(0, RIM), :], rim_c.at[f, 1, pl.ds(RIM * xd, RIM)],
                halo_send.at[2], c_sem, (gx_to, gy_dn)))

    for copy in faces + corners + smalls[2:]:
        copy.start()
    for d in range(1, 16):
        remote(ownid, ids.at[gy], id_send, id_sem, (gx, lax.rem(gy + d, n_gy))).start()

    @pl.loop(1, 7)
    def _(c):
        sweep_inner(c, range(1, GROUPS - 1), range(2, GROUPS - 2))
        for k in range(1, 7):
            pl.when(c == k)(functools.partial(hop1, k, 0))

    ids[gy] = mine[:1]

    pltpu.make_async_copy(rim_y, rim_y, y_sem).wait()
    for copy in smalls[:2]:
        copy.wait_recv()

    def unpack(zone, tiles):
        for tile in tiles:
            for c in range(3):
                coef[zone, tile, c] = jnp.broadcast_to(packs[zone, tile, pl.ds(c, 1), :], (8, DEPTH))

    unpack(1, (0, 3))

    def rims(source, lo, n, off):
        @pl.loop(0, n)
        def _(i):
            for f in range(2):
                lev[0, f, lo + i, pl.ds(RIM, RIM), :] = source[f, 0, off + i]
                lev[0, f, lo + i, pl.ds(8 + 2 * EDGE, RIM), :] = source[f, 1, off + i]

    rims(rim_y, RIM, EDGE, 0)

    @pl.loop(1, 7)
    def _(c):
        sweep_inner(c, (0, 1, GROUPS - 2, GROUPS - 1), (1, GROUPS - 2))
        for k in range(1, 7):
            pl.when(c == k)(functools.partial(hop1, k, 1))

    others = ids.at[pl.ds(0, n_gy - 1)]
    pltpu.make_async_copy(others, others, id_sem).wait()
    total = ids[0]
    for s in range(1, 16):
        total = total + ids[s]
    both = jnp.broadcast_to(total, (n_gy, DEPTH))
    lanes = lax.broadcasted_iota(jnp.int32, (n_gy, DEPTH), 1)
    wanted = gx * n_gy + lax.broadcasted_iota(jnp.int32, (n_gy, DEPTH), 0)
    match = (both == wanted) & (lanes < 2 * n_gy)
    least = jnp.min(jnp.where(match, lanes, 2 * n_gy - 1), axis=1, keepdims=True)
    most = jnp.max(jnp.where(match, lanes, 0), axis=1, keepdims=True)
    table_v[0] = jnp.broadcast_to(least, (n_gy, DEPTH))
    table_v[1] = jnp.broadcast_to(most, (n_gy, DEPTH))
    tab = pltpu.make_async_copy(table_v, table_s, tab_sem)
    tab.start()

    for copy in faces:
        copy.wait_recv()
    for copy in smalls[2:]:
        copy.wait_recv()
    unpack(0, range(4))
    unpack(2, range(4))
    pltpu.make_async_copy(rim_c, rim_c, c_sem).wait()
    rims(rim_c, 0, RIM, 0)
    rims(rim_c, RIM + EDGE, RIM, RIM)

    @pl.loop(0, 2)
    def _(e):
        sweep(
            28 * e, range(GROUPS), range(1, GROUPS - 1),
            lambda level: 1 + 34 * e + level * (1 - 2 * e), lambda level: 2,
        )
        for k in range(2):
            @pl.when(e == k)
            def _():
                hop1(7 * k, 0)
                hop1(7 * k, 1)

    tab.wait()
    for c in ORDER:
        hop2(c)

    pltpu.make_async_copy(out, out, out_sem).wait()
    for k, sent in enumerate((rim_y, fin.at[0, 0], rim_c)):
        pltpu.make_async_copy(sent, sent, halo_send.at[k]).wait()
    for copy in smalls:
        copy.wait_send()
    pltpu.make_async_copy(others, others, id_send).wait()
    for c in range(CHUNKS):
        some = recv[c].at[pl.ds(0, 2 * n_gy - 2)]
        pltpu.make_async_copy(some, some, hop1_send.at[c]).wait()
        pltpu.make_async_copy(some, some, hop2_send.at[c]).wait()


def per_device(n_gx, n_gy, phase, solute, undercool, mobility, diffusivity, owner):
    smem = pl.BlockSpec(memory_space=pltpu.SMEM)
    hbm = pl.BlockSpec(memory_space=pl.ANY)
    f32 = jnp.float32
    dma = pltpu.SemaphoreType.DMA
    out = pl.pallas_call(
        functools.partial(kernel, n_gx, n_gy),
        out_shape=pltpu.VMEM((2, 2, 16, 2, EDGE, DEPTH), f32),
        in_specs=[hbm, hbm, smem, smem, smem, smem],
        out_specs=hbm,
        scratch_shapes=[
            pltpu.VMEM((NSTEPS, 2, EDGE + 2 * RIM, 8 * GROUPS, DEPTH), f32),
            pltpu.VMEM((2, 2, 16, 2, EDGE, DEPTH), f32),
            pltpu.VMEM((2, 2, EDGE, RIM, DEPTH), f32),
            pltpu.VMEM((2, 2, 2 * RIM, RIM, DEPTH), f32),
            pltpu.VMEM((3, 4, 3, 8, DEPTH), f32),
            pltpu.VMEM((3, 4, 8, DEPTH), f32),
            pltpu.VMEM((2, 8, DEPTH), f32),
            pltpu.VMEM((1, DEPTH), jnp.int32),
            pltpu.VMEM((n_gy, 1, DEPTH), jnp.int32),
            pltpu.VMEM((2, n_gy, DEPTH), jnp.int32),
            pltpu.SMEM((2, n_gy, DEPTH), jnp.int32),
            pltpu.VMEM((CHUNKS, n_gy, 2, 2, 8, DEPTH), f32),
        ]
        + [pltpu.VMEM((2 * n_gy, 2, 8, DEPTH), f32)] * CHUNKS
        + [
            dma((4,)), dma(()), dma((2, 2, 2)), dma(()), dma((8,)), dma(()), dma(()), dma((CHUNKS,)), dma(()),
            dma((3,)), dma((8,)), dma(()), dma((CHUNKS,)), dma((CHUNKS,)),
        ],
        compiler_params=pltpu.CompilerParams(
            collective_id=0, has_side_effects=True, vmem_limit_bytes=56 << 20
        ),
    )(phase, solute, undercool, mobility, diffusivity, owner)
    shape = (1, 2, EDGE, EDGE, DEPTH)
    return out[0].reshape(shape), out[1].reshape(shape)


def solution(mesh):
    in_specs = (
        P("gx", "gy", None, None, None),
        P("gx", "gy", None, None, None),
        P("gx", "gy"),
        P("gx", "gy"),
        P("gx", "gy"),
        P("gx", "gy"),
    )
    out_specs = (P(("gx", "gy"), None, None, None, None), P(("gx", "gy"), None, None, None, None))
    return jax.shard_map(
        functools.partial(per_device, mesh.shape["gx"], mesh.shape["gy"]),
        mesh=mesh, in_specs=in_specs, out_specs=out_specs, check_vma=False,
    )
```

```python
import functools

import jax
import jax.numpy as jnp
from jax import lax
from jax.experimental import pallas as pl
from jax.experimental.pallas import tpu as pltpu
from jax.sharding import PartitionSpec as P

MESH = pl.DeviceIdType.MESH
NSTEPS = 4
RIM = 4
EDGE = 32
DEPTH = 128
GROUPS = 10
CHUNKS = 8
ORDER = (1, 2, 3, 4, 5, 6, 0, 7)

aniso_strength = 0.05
coupling = 2.0


def kernel(
    n_gx, n_gy,
    phase, solute, under, mobile, spread_in, owner,
    out,
    under_s, mobile_s, spread_s, owner_s, small_sem,
    lev, fin, rim_y, rim_c, coef, packs, own, ownid, ids, table_v, table_s, stage,
    recv0, recv1, recv2, recv3, recv4, recv5, recv6, recv7,
    in_sem, y_sem, x_sem, c_sem, coef_sem, id_sem, tab_sem, hop1_sem, out_sem,
    halo_send, coef_send, id_send, hop1_send, hop2_send,
):
    recv = (recv0, recv1, recv2, recv3, recv4, recv5, recv6, recv7)
    fields = (phase, solute)
    gx = lax.axis_index("gx")
    gy = lax.axis_index("gy")
    gx_up = lax.rem(gx + 1, n_gx)
    gx_dn = lax.rem(gx + n_gx - 1, n_gx)
    gy_up = lax.rem(gy + 1, n_gy)
    gy_dn = lax.rem(gy + n_gy - 1, n_gy)

    def remote(src, dst, send, recv_sem, device):
        return pltpu.make_async_remote_copy(
            src_ref=src, dst_ref=dst, send_sem=send, recv_sem=recv_sem,
            device_id=device, device_id_type=MESH,
        )

    loads = []
    for f in range(2):
        for b in range(2):
            loads.append(pltpu.make_async_copy(
                fields[f].at[0, b],
                lev.at[0, f, pl.ds(RIM, EDGE), pl.ds(8 + EDGE * b, EDGE), :],
                in_sem.at[2 * f + b],
            ))
    scalars = [
        pltpu.make_async_copy(src, dst, small_sem.at[k])
        for k, (src, dst) in enumerate(((under, under_s), (mobile, mobile_s), (spread_in, spread_s), (owner, owner_s)))
    ]
    for copy in scalars:
        copy.start()

    barrier = pltpu.get_barrier_semaphore()

    for d in range(1, 16):
        pl.semaphore_signal(barrier, inc=1, device_id=(gx, lax.rem(gy + d, n_gy)), device_id_type=MESH)

    for device in ((gx_up, gy), (gx_dn, gy), (gx_up, gy_up), (gx_up, gy_dn), (gx_dn, gy_up), (gx_dn, gy_dn)):
        pl.semaphore_signal(barrier, inc=1, device_id=device, device_id_type=MESH)

    for copy in loads:
        copy.start()

    for copy in scalars:
        copy.wait()
    line = lax.broadcasted_iota(jnp.int32, (8, DEPTH), 0)
    for b in range(2):
        packed = jnp.zeros((8, DEPTH), jnp.float32)
        for c, values in enumerate((under_s, mobile_s, spread_s)):
            block = jnp.full((8, DEPTH), values[0, b], jnp.float32)
            packed = jnp.where(line == c, block, packed)
            coef[1, 1 + b, c] = block
        own[b] = packed
    lane = lax.broadcasted_iota(jnp.int32, (8, DEPTH), 1)
    mine = jnp.where(lane == 2 * gy, owner_s[0, 0], 0) + jnp.where(lane == 2 * gy + 1, owner_s[0, 1], 0)
    ownid[...] = mine[:1]

    first_lane = lane == 0
    last_lane = lane == DEPTH - 1

    def advance(level, i, q):
        near = []
        for f in range(2):
            low = 8 * q
            mid = lev[level, f, i, pl.ds(low, 8), :]
            lower_x = lev[level, f, i - 1, pl.ds(low, 8), :]
            upper_x = lev[level, f, i + 1, pl.ds(low, 8), :]
            lower_y = pltpu.roll(mid, 1, 0) if q == 0 else lev[level, f, i, pl.ds(low - 1, 8), :]
            upper_y = pltpu.roll(mid, 7, 0) if q == GROUPS - 1 else lev[level, f, i, pl.ds(low + 1, 8), :]
            lower_z = jnp.where(first_lane, mid, pltpu.roll(mid, 1, 1))
            upper_z = jnp.where(last_lane, mid, pltpu.roll(mid, DEPTH - 1, 1))
            near.append((mid, lower_x, upper_x, lower_y, upper_y, lower_z, upper_z))
        zone = (i + EDGE - RIM) // EDGE
        tile = (q + 3) // 4
        under = coef[zone, tile, 0]
        mobile = coef[zone, tile, 1]
        spread = coef[zone, tile, 2]
        p, xl, xu, yl, yu, zl, zu = near[0]
        u, sxl, sxu, syl, syu, szl, szu = near[1]
        dx, dy, dz = xu - xl, yu - yl, zu - zl
        dx2, dy2, dz2 = dx * dx, dy * dy, dz * dz
        two = dx2 + dy2 + dz2
        four = dx2 * dx2 + dy2 * dy2 + dz2 * dz2
        base = two + 4.0
        top = (4.0 * aniso_strength) * four - (3.0 * aniso_strength) * (two * two)
        aniso = 1.0 + top / (base * base)
        lap = (xu + xl) + (yu + yl) + (zu + zl) - 6.0 * p
        lap_u = (sxu + sxl) + (syu + syl) + (szu + szl) - 6.0 * u
        well = 1.0 - p * p
        change = mobile * (aniso * lap + p * well - coupling * (well * well) * (under + u))
        return p + change, u + spread * lap_u + 0.5 * change

    def sweep(first, groups, last_groups, starts, pairs):
        @pl.loop(0, NSTEPS - 1)
        def _(level):
            @pl.loop(0, pairs(level))
            def _(n):
                for m in range(2):
                    i = starts(level) + 2 * n + m
                    for q in groups:
                        new_p, new_u = advance(level, i, q)
                        lev[level + 1, 0, i, pl.ds(8 * q, 8), :] = new_p
                        lev[level + 1, 1, i, pl.ds(8 * q, 8), :] = new_u

        @pl.loop(0, 2)
        def _(n):
            for m in range(2):
                i = first + RIM + 2 * n + m
                for q in last_groups:
                    b, g = (q - 1) // 4, (q - 1) % 4
                    new_p, new_u = advance(NSTEPS - 1, i, q)
                    fin[0, b, first // 2 + n, m, pl.ds(8 * g, 8), :] = new_p
                    fin[1, b, first // 2 + n, m, pl.ds(8 * g, 8), :] = new_u

    def sweep_inner(c, groups, last_groups):
        opening = 1 - (c + 3) // 5
        sweep(
            4 * c, groups, last_groups,
            lambda level: 4 * c + 7 - level - opening * (6 - 2 * level), lambda level: 2 + opening * (3 - level),
        )

    z, y = gy // 4, lax.rem(gy, 4)
    parity = lax.rem(z + y, 2)
    half = y // 2

    def piece(to_z, to_y, odd):
        side = to_y // 2
        g = 3 * side if odd else 1 + side
        return lax.rem(to_z, 2), pl.multiple_of(8 * g, 8), to_z // 2

    def hop1(c, odd):
        for dz in range(4):
            to_z = lax.rem(z + dz, 4)
            for m in range(2):
                to_y = 2 * lax.rem(half + m, 2) + lax.rem(to_z + odd + c, 2)
                f, row, h = piece(to_z, to_y, odd)
                src = fin.at[f, :, pl.ds(2 * c, 2), h, pl.ds(row, 8), :]
                dst = recv[c].at[pl.ds(2 * gy, 2)]

                def away():
                    remote(src, dst, hop1_send.at[c], hop1_sem.at[c], (gx, 4 * to_z + to_y)).start()

                if dz == 0 and m == 0:
                    pl.when(parity != (odd + c) % 2)(away)

                    @pl.when(parity == (odd + c) % 2)
                    def _():
                        pltpu.make_async_copy(src, dst, hop1_sem.at[c]).start()
                else:
                    away()

    my_f, my_h = lax.rem(z, 2), z // 2

    def hop2(c):
        pltpu.make_async_copy(recv[c], recv[c], hop1_sem.at[c]).wait()
        odd = lax.rem(parity + c, 2)
        row = pl.multiple_of(8 * ((1 - odd) * (1 + half) + odd * 3 * half), 8)
        dst = out.at[my_f, :, pl.ds(2 * c, 2), my_h, pl.ds(row, 8), :]
        for dz in range(4):
            for dy in range(4):
                to = 4 * lax.rem(z + dz, 4) + lax.rem(y + dy, 4)
                for j in range(2):
                    stage[c, to, j] = recv[c][table_s[j, to, 0]]
                if dz or dy:
                    remote(stage.at[c, to], dst, hop2_send.at[c], out_sem, (gx, to)).start()
                else:
                    pltpu.make_async_copy(stage.at[c, to], dst, out_sem).start()

    pl.semaphore_wait(barrier, n_gy + 5)

    for f in range(2):
        remote(fields[f].at[0, 1, :, pl.ds(EDGE - RIM, RIM), :], rim_y.at[f, 0], halo_send.at[0], y_sem, (gx, gy_up)).start()
        remote(fields[f].at[0, 0, :, pl.ds(0, RIM), :], rim_y.at[f, 1], halo_send.at[0], y_sem, (gx, gy_dn)).start()
    smalls = [
        remote(own.at[1], packs.at[1, 0], coef_send.at[0], coef_sem.at[0], (gx, gy_up)),
        remote(own.at[0], packs.at[1, 3], coef_send.at[1], coef_sem.at[1], (gx, gy_dn)),
        remote(own.at[pl.ds(0, 2)], packs.at[0, pl.ds(1, 2)], coef_send.at[2], coef_sem.at[2], (gx_up, gy)),
        remote(own.at[pl.ds(0, 2)], packs.at[2, pl.ds(1, 2)], coef_send.at[3], coef_sem.at[3], (gx_dn, gy)),
        remote(own.at[1], packs.at[0, 0], coef_send.at[4], coef_sem.at[4], (gx_up, gy_up)),
        remote(own.at[0], packs.at[0, 3], coef_send.at[5], coef_sem.at[5], (gx_up, gy_dn)),
        remote(own.at[1], packs.at[2, 0], coef_send.at[6], coef_sem.at[6], (gx_dn, gy_up)),
        remote(own.at[0], packs.at[2, 3], coef_send.at[7], coef_sem.at[7], (gx_dn, gy_dn)),
    ]
    for copy in smalls[:2]:
        copy.start()
    for copy in loads:
        copy.wait()
    faces = []
    for f in range(2):
        for b in range(2):
            rows = pl.ds(8 + EDGE * b, EDGE)
            faces.append(remote(
                fields[f].at[0, b, pl.ds(EDGE - RIM, RIM)], lev.at[0, f, pl.ds(0, RIM), rows, :],
                halo_send.at[1], x_sem.at[0, f, b], (gx_up, gy)))
            faces.append(remote(
                fields[f].at[0, b, pl.ds(0, RIM)], lev.at[0, f, pl.ds(RIM + EDGE, RIM), rows, :],
                halo_send.at[1], x_sem.at[1, f, b], (gx_dn, gy)))
    corners = []
    for f in range(2):
        for xd, (planes, gx_to) in enumerate(((pl.ds(EDGE - RIM, RIM), gx_up), (pl.ds(0, RIM), gx_dn))):
            corners.append(remote(
                fields[f].at[0, 1, planes, pl.ds(EDGE - RIM, RIM), :], rim_c.at[f, 0, pl.ds(RIM * xd, RIM)],
                halo_send.at[2], c_sem, (gx_to, gy_up)))
            corners.append(remote(
                fields[f].at[0, 0, planes, pl.ds(0, RIM), :], rim_c.at[f, 1, pl.ds(RIM * xd, RIM)],
                halo_send.at[2], c_sem, (gx_to, gy_dn)))

    for copy in faces + corners + smalls[2:]:
        copy.start()
    for d in range(1, 16):
        remote(ownid, ids.at[gy], id_send, id_sem, (gx, lax.rem(gy + d, n_gy))).start()

    @pl.loop(1, 7)
    def _(c):
        sweep_inner(c, range(1, GROUPS - 1), range(2, GROUPS - 2))
        for k in range(1, 7):
            pl.when(c == k)(functools.partial(hop1, k, 0))

    ids[gy] = mine[:1]

    pltpu.make_async_copy(rim_y, rim_y, y_sem).wait()
    for copy in smalls[:2]:
        copy.wait_recv()

    def unpack(zone, tiles):
        for tile in tiles:
            for c in range(3):
                coef[zone, tile, c] = jnp.broadcast_to(packs[zone, tile, pl.ds(c, 1), :], (8, DEPTH))

    unpack(1, (0, 3))

    def rims(source, lo, n, off):
        @pl.loop(0, n)
        def _(i):
            for f in range(2):
                lev[0, f, lo + i, pl.ds(RIM, RIM), :] = source[f, 0, off + i]
                lev[0, f, lo + i, pl.ds(8 + 2 * EDGE, RIM), :] = source[f, 1, off + i]

    rims(rim_y, RIM, EDGE, 0)

    @pl.loop(1, 7)
    def _(c):
        sweep_inner(c, (0, 1, GROUPS - 2, GROUPS - 1), (1, GROUPS - 2))
        for k in range(1, 7):
            pl.when(c == k)(functools.partial(hop1, k, 1))

    others = ids.at[pl.ds(0, n_gy - 1)]
    pltpu.make_async_copy(others, others, id_sem).wait()
    total = ids[0]
    for s in range(1, 16):
        total = total + ids[s]
    both = jnp.broadcast_to(total, (n_gy, DEPTH))
    lanes = lax.broadcasted_iota(jnp.int32, (n_gy, DEPTH), 1)
    wanted = gx * n_gy + lax.broadcasted_iota(jnp.int32, (n_gy, DEPTH), 0)
    match = (both == wanted) & (lanes < 2 * n_gy)
    least = jnp.min(jnp.where(match, lanes, 2 * n_gy - 1), axis=1, keepdims=True)
    most = jnp.max(jnp.where(match, lanes, 0), axis=1, keepdims=True)
    table_v[0] = jnp.broadcast_to(least, (n_gy, DEPTH))
    table_v[1] = jnp.broadcast_to(most, (n_gy, DEPTH))
    tab = pltpu.make_async_copy(table_v, table_s, tab_sem)
    tab.start()

    for copy in faces:
        copy.wait_recv()
    for copy in smalls[2:]:
        copy.wait_recv()
    unpack(0, range(4))
    unpack(2, range(4))
    pltpu.make_async_copy(rim_c, rim_c, c_sem).wait()
    rims(rim_c, 0, RIM, 0)
    rims(rim_c, RIM + EDGE, RIM, RIM)

    @pl.loop(0, 2)
    def _(e):
        sweep(
            28 * e, range(GROUPS), range(1, GROUPS - 1),
            lambda level: 1 + 34 * e + level * (1 - 2 * e), lambda level: 2,
        )
        for k in range(2):
            @pl.when(e == k)
            def _():
                hop1(7 * k, 0)
                hop1(7 * k, 1)

    tab.wait()
    for c in ORDER:
        hop2(c)

    pltpu.make_async_copy(out, out, out_sem).wait()
    for k, sent in enumerate((rim_y, fin.at[0, 0], rim_c)):
        pltpu.make_async_copy(sent, sent, halo_send.at[k]).wait()
    for copy in smalls:
        copy.wait_send()
    pltpu.make_async_copy(others, others, id_send).wait()
    for c in range(CHUNKS):
        some = recv[c].at[pl.ds(0, 2 * n_gy - 2)]
        pltpu.make_async_copy(some, some, hop1_send.at[c]).wait()
        pltpu.make_async_copy(some, some, hop2_send.at[c]).wait()


def per_device(n_gx, n_gy, phase, solute, undercool, mobility, diffusivity, owner):
    hbm = pl.BlockSpec(memory_space=pl.ANY)
    f32 = jnp.float32
    dma = pltpu.SemaphoreType.DMA
    out = pl.pallas_call(
        functools.partial(kernel, n_gx, n_gy),
        out_shape=pltpu.VMEM((2, 2, 16, 2, EDGE, DEPTH), f32),
        in_specs=[hbm] * 6,
        out_specs=hbm,
        scratch_shapes=[
            pltpu.SMEM((1, 2), f32), pltpu.SMEM((1, 2), f32), pltpu.SMEM((1, 2), f32), pltpu.SMEM((1, 2), jnp.int32), dma((4,)),
            pltpu.VMEM((NSTEPS, 2, EDGE + 2 * RIM, 8 * GROUPS, DEPTH), f32),
            pltpu.VMEM((2, 2, 16, 2, EDGE, DEPTH), f32),
            pltpu.VMEM((2, 2, EDGE, RIM, DEPTH), f32),
            pltpu.VMEM((2, 2, 2 * RIM, RIM, DEPTH), f32),
            pltpu.VMEM((3, 4, 3, 8, DEPTH), f32),
            pltpu.VMEM((3, 4, 8, DEPTH), f32),
            pltpu.VMEM((2, 8, DEPTH), f32),
            pltpu.VMEM((1, DEPTH), jnp.int32),
            pltpu.VMEM((n_gy, 1, DEPTH), jnp.int32),
            pltpu.VMEM((2, n_gy, DEPTH), jnp.int32),
            pltpu.SMEM((2, n_gy, DEPTH), jnp.int32),
            pltpu.VMEM((CHUNKS, n_gy, 2, 2, 8, DEPTH), f32),
        ]
        + [pltpu.VMEM((2 * n_gy, 2, 8, DEPTH), f32)] * CHUNKS
        + [
            dma((4,)), dma(()), dma((2, 2, 2)), dma(()), dma((8,)), dma(()), dma(()), dma((CHUNKS,)), dma(()),
            dma((3,)), dma((8,)), dma(()), dma((CHUNKS,)), dma((CHUNKS,)),
        ],
        compiler_params=pltpu.CompilerParams(
            collective_id=0, has_side_effects=True, vmem_limit_bytes=56 << 20
        ),
    )(phase, solute, undercool, mobility, diffusivity, owner)
    shape = (1, 2, EDGE, EDGE, DEPTH)
    return out[0].reshape(shape), out[1].reshape(shape)


def solution(mesh):
    in_specs = (
        P("gx", "gy", None, None, None),
        P("gx", "gy", None, None, None),
        P("gx", "gy"),
        P("gx", "gy"),
        P("gx", "gy"),
        P("gx", "gy"),
    )
    out_specs = (P(("gx", "gy"), None, None, None, None), P(("gx", "gy"), None, None, None, None))
    return jax.shard_map(
        functools.partial(per_device, mesh.shape["gx"], mesh.shape["gy"]),
        mesh=mesh, in_specs=in_specs, out_specs=out_specs, check_vma=False,
    )
```

```python
import functools

import jax
import jax.numpy as jnp
from jax import lax
from jax.experimental import pallas as pl
from jax.experimental.pallas import tpu as pltpu
from jax.sharding import PartitionSpec as P

MESH = pl.DeviceIdType.MESH
NSTEPS = 4
RIM = 4
EDGE = 32
DEPTH = 128
GROUPS = 10
CHUNKS = 8
ORDER = (1, 2, 3, 4, 5, 6, 0, 7)

aniso_strength = 0.05
coupling = 2.0


def kernel(
    n_gx, n_gy,
    phase, solute, under, mobile, spread_in, owner,
    out,
    under_s, mobile_s, spread_s, owner_s, small_sem,
    lev, fin, rim_y, rim_c, coef, packs, own, ownid, ids, table_v, table_s, stage,
    recv0, recv1, recv2, recv3, recv4, recv5, recv6, recv7,
    in_sem, y_sem, x_sem, c_sem, coef_sem, id_sem, tab_sem, hop1_sem, out_sem,
    halo_send, coef_send, id_send, hop1_send, hop2_send,
):
    recv = (recv0, recv1, recv2, recv3, recv4, recv5, recv6, recv7)
    fields = (phase, solute)
    gx = lax.axis_index("gx")
    gy = lax.axis_index("gy")
    gx_up = lax.rem(gx + 1, n_gx)
    gx_dn = lax.rem(gx + n_gx - 1, n_gx)
    gy_up = lax.rem(gy + 1, n_gy)
    gy_dn = lax.rem(gy + n_gy - 1, n_gy)

    def remote(src, dst, send, recv_sem, device):
        return pltpu.make_async_remote_copy(
            src_ref=src, dst_ref=dst, send_sem=send, recv_sem=recv_sem,
            device_id=device, device_id_type=MESH,
        )

    loads = []
    for f in range(2):
        for b in range(2):
            loads.append(pltpu.make_async_copy(
                fields[f].at[0, b],
                lev.at[0, f, pl.ds(RIM, EDGE), pl.ds(8 + EDGE * b, EDGE), :],
                in_sem.at[2 * f + b],
            ))
    scalars = [
        pltpu.make_async_copy(src, dst, small_sem.at[k])
        for k, (src, dst) in enumerate(((under, under_s), (mobile, mobile_s), (spread_in, spread_s), (owner, owner_s)))
    ]
    for copy in scalars:
        copy.start()

    barrier = pltpu.get_barrier_semaphore()

    for d in range(1, 16):
        pl.semaphore_signal(barrier, inc=1, device_id=(gx, lax.rem(gy + d, n_gy)), device_id_type=MESH)

    for device in ((gx_up, gy), (gx_dn, gy), (gx_up, gy_up), (gx_up, gy_dn), (gx_dn, gy_up), (gx_dn, gy_dn)):
        pl.semaphore_signal(barrier, inc=1, device_id=device, device_id_type=MESH)

    for copy in loads:
        copy.start()

    for copy in scalars:
        copy.wait()
    line = lax.broadcasted_iota(jnp.int32, (8, DEPTH), 0)
    for b in range(2):
        packed = jnp.zeros((8, DEPTH), jnp.float32)
        for c, values in enumerate((under_s, mobile_s, spread_s)):
            block = jnp.full((8, DEPTH), values[0, b], jnp.float32)
            packed = jnp.where(line == c, block, packed)
            coef[1, 1 + b, c] = block
        own[b] = packed
    lane = lax.broadcasted_iota(jnp.int32, (8, DEPTH), 1)
    mine = jnp.where(lane == 2 * gy, owner_s[0, 0], 0) + jnp.where(lane == 2 * gy + 1, owner_s[0, 1], 0)
    ownid[...] = mine[:1]

    first_lane = lane == 0
    last_lane = lane == DEPTH - 1

    def advance(level, i, q):
        near = []
        for f in range(2):
            low = 8 * q
            mid = lev[level, f, i, pl.ds(low, 8), :]
            lower_x = lev[level, f, i - 1, pl.ds(low, 8), :]
            upper_x = lev[level, f, i + 1, pl.ds(low, 8), :]
            lower_y = pltpu.roll(mid, 1, 0) if q == 0 else lev[level, f, i, pl.ds(low - 1, 8), :]
            upper_y = pltpu.roll(mid, 7, 0) if q == GROUPS - 1 else lev[level, f, i, pl.ds(low + 1, 8), :]
            lower_z = jnp.where(first_lane, mid, pltpu.roll(mid, 1, 1))
            upper_z = jnp.where(last_lane, mid, pltpu.roll(mid, DEPTH - 1, 1))
            near.append((mid, lower_x, upper_x, lower_y, upper_y, lower_z, upper_z))
        zone = (i + EDGE - RIM) // EDGE
        tile = (q + 3) // 4
        under = coef[zone, tile, 0]
        mobile = coef[zone, tile, 1]
        spread = coef[zone, tile, 2]
        p, xl, xu, yl, yu, zl, zu = near[0]
        u, sxl, sxu, syl, syu, szl, szu = near[1]
        dx, dy, dz = xu - xl, yu - yl, zu - zl
        dx2, dy2, dz2 = dx * dx, dy * dy, dz * dz
        two = dx2 + dy2 + dz2
        four = dx2 * dx2 + dy2 * dy2 + dz2 * dz2
        base = two + 4.0
        top = (4.0 * aniso_strength) * four - (3.0 * aniso_strength) * (two * two)
        aniso = 1.0 + top / (base * base)
        lap = (xu + xl) + (yu + yl) + (zu + zl) - 6.0 * p
        lap_u = (sxu + sxl) + (syu + syl) + (szu + szl) - 6.0 * u
        well = 1.0 - p * p
        change = mobile * (aniso * lap + p * well - coupling * (well * well) * (under + u))
        return p + change, u + spread * lap_u + 0.5 * change

    def sweep(first, groups, last_groups, starts, pairs):
        @pl.loop(0, NSTEPS - 1)
        def _(level):
            @pl.loop(0, pairs(level))
            def _(n):
                for m in range(2):
                    i = starts(level) + 2 * n + m
                    for q in groups:
                        new_p, new_u = advance(level, i, q)
                        lev[level + 1, 0, i, pl.ds(8 * q, 8), :] = new_p
                        lev[level + 1, 1, i, pl.ds(8 * q, 8), :] = new_u

        @pl.loop(0, 2)
        def _(n):
            for m in range(2):
                i = first + RIM + 2 * n + m
                for q in last_groups:
                    b, g = (q - 1) // 4, (q - 1) % 4
                    new_p, new_u = advance(NSTEPS - 1, i, q)
                    fin[0, b, first // 2 + n, m, pl.ds(8 * g, 8), :] = new_p
                    fin[1, b, first // 2 + n, m, pl.ds(8 * g, 8), :] = new_u

    def sweep_inner(c, groups, last_groups):
        opening = 1 - (c + 3) // 5
        sweep(
            4 * c, groups, last_groups,
            lambda level: 4 * c + 7 - level - opening * (6 - 2 * level), lambda level: 2 + opening * (3 - level),
        )

    z, y = gy // 4, lax.rem(gy, 4)
    parity = lax.rem(z + y, 2)
    half = y // 2

    def piece(to_z, to_y, odd):
        side = to_y // 2
        g = 3 * side if odd else 1 + side
        return lax.rem(to_z, 2), pl.multiple_of(8 * g, 8), to_z // 2

    def hop1(c, odd):
        for dz in range(4):
            to_z = lax.rem(z + dz, 4)
            for m in range(2):
                to_y = 2 * lax.rem(half + m, 2) + lax.rem(to_z + odd + c, 2)
                f, row, h = piece(to_z, to_y, odd)
                src = fin.at[f, :, pl.ds(2 * c, 2), h, pl.ds(row, 8), :]
                dst = recv[c].at[pl.ds(2 * gy, 2)]

                def away():
                    remote(src, dst, hop1_send.at[c], hop1_sem.at[c], (gx, 4 * to_z + to_y)).start()

                if dz == 0 and m == 0:
                    pl.when(parity != (odd + c) % 2)(away)

                    @pl.when(parity == (odd + c) % 2)
                    def _():
                        pltpu.make_async_copy(src, dst, hop1_sem.at[c]).start()
                else:
                    away()

    my_f, my_h = lax.rem(z, 2), z // 2

    def hop2(c):
        pltpu.make_async_copy(recv[c], recv[c], hop1_sem.at[c]).wait()
        odd = lax.rem(parity + c, 2)
        row = pl.multiple_of(8 * ((1 - odd) * (1 + half) + odd * 3 * half), 8)
        dst = out.at[my_f, :, pl.ds(2 * c, 2), my_h, pl.ds(row, 8), :]
        def pick(d):
            to = lax.rem(gy + d, n_gy)
            for j in range(2):
                stage[c, to, j] = recv[c][table_s[j, to, 0]]
            return to

        @pl.loop(0, 5)
        def _(n):
            for m in range(3):
                to = pick(3 * n + m + 1)
                remote(stage.at[c, to], dst, hop2_send.at[c], out_sem, (gx, to)).start()

        to = pick(0)
        pltpu.make_async_copy(stage.at[c, to], dst, out_sem).start()

    pl.semaphore_wait(barrier, n_gy + 5)

    for f in range(2):
        remote(fields[f].at[0, 1, :, pl.ds(EDGE - RIM, RIM), :], rim_y.at[f, 0], halo_send.at[0], y_sem, (gx, gy_up)).start()
        remote(fields[f].at[0, 0, :, pl.ds(0, RIM), :], rim_y.at[f, 1], halo_send.at[0], y_sem, (gx, gy_dn)).start()
    smalls = [
        remote(own.at[1], packs.at[1, 0], coef_send.at[0], coef_sem.at[0], (gx, gy_up)),
        remote(own.at[0], packs.at[1, 3], coef_send.at[1], coef_sem.at[1], (gx, gy_dn)),
        remote(own.at[pl.ds(0, 2)], packs.at[0, pl.ds(1, 2)], coef_send.at[2], coef_sem.at[2], (gx_up, gy)),
        remote(own.at[pl.ds(0, 2)], packs.at[2, pl.ds(1, 2)], coef_send.at[3], coef_sem.at[3], (gx_dn, gy)),
        remote(own.at[1], packs.at[0, 0], coef_send.at[4], coef_sem.at[4], (gx_up, gy_up)),
        remote(own.at[0], packs.at[0, 3], coef_send.at[5], coef_sem.at[5], (gx_up, gy_dn)),
        remote(own.at[1], packs.at[2, 0], coef_send.at[6], coef_sem.at[6], (gx_dn, gy_up)),
        remote(own.at[0], packs.at[2, 3], coef_send.at[7], coef_sem.at[7], (gx_dn, gy_dn)),
    ]
    for copy in smalls[:2]:
        copy.start()
    for copy in loads:
        copy.wait()
    faces = []
    for f in range(2):
        for b in range(2):
            rows = pl.ds(8 + EDGE * b, EDGE)
            faces.append(remote(
                fields[f].at[0, b, pl.ds(EDGE - RIM, RIM)], lev.at[0, f, pl.ds(0, RIM), rows, :],
                halo_send.at[1], x_sem.at[0, f, b], (gx_up, gy)))
            faces.append(remote(
                fields[f].at[0, b, pl.ds(0, RIM)], lev.at[0, f, pl.ds(RIM + EDGE, RIM), rows, :],
                halo_send.at[1], x_sem.at[1, f, b], (gx_dn, gy)))
    corners = []
    for f in range(2):
        for xd, (planes, gx_to) in enumerate(((pl.ds(EDGE - RIM, RIM), gx_up), (pl.ds(0, RIM), gx_dn))):
            corners.append(remote(
                fields[f].at[0, 1, planes, pl.ds(EDGE - RIM, RIM), :], rim_c.at[f, 0, pl.ds(RIM * xd, RIM)],
                halo_send.at[2], c_sem, (gx_to, gy_up)))
            corners.append(remote(
                fields[f].at[0, 0, planes, pl.ds(0, RIM), :], rim_c.at[f, 1, pl.ds(RIM * xd, RIM)],
                halo_send.at[2], c_sem, (gx_to, gy_dn)))

    for copy in faces + corners + smalls[2:]:
        copy.start()
    for d in range(1, 16):
        remote(ownid, ids.at[gy], id_send, id_sem, (gx, lax.rem(gy + d, n_gy))).start()

    @pl.loop(1, 7)
    def _(c):
        sweep_inner(c, range(1, GROUPS - 1), (2, 3, 6, 7))
        for k in range(1, 7):
            pl.when(c == k)(functools.partial(hop1, k, 0))

    ids[gy] = mine[:1]

    pltpu.make_async_copy(rim_y, rim_y, y_sem).wait()
    for copy in smalls[:2]:
        copy.wait_recv()

    def unpack(zone, tiles):
        for tile in tiles:
            for c in range(3):
                coef[zone, tile, c] = jnp.broadcast_to(packs[zone, tile, pl.ds(c, 1), :], (8, DEPTH))

    unpack(1, (0, 3))

    def rims(source, lo, n, off):
        @pl.loop(0, n)
        def _(i):
            for f in range(2):
                lev[0, f, lo + i, pl.ds(RIM, RIM), :] = source[f, 0, off + i]
                lev[0, f, lo + i, pl.ds(8 + 2 * EDGE, RIM), :] = source[f, 1, off + i]

    rims(rim_y, RIM, EDGE, 0)

    @pl.loop(1, 7)
    def _(c):
        sweep_inner(c, (0, 1, GROUPS - 2, GROUPS - 1), (1, 4, 5, 8))
        for k in range(1, 7):
            pl.when(c == k)(functools.partial(hop1, k, 1))

    for copy in faces:
        copy.wait_recv()
    for copy in smalls[2:]:
        copy.wait_recv()
    unpack(0, range(4))
    unpack(2, range(4))
    pltpu.make_async_copy(rim_c, rim_c, c_sem).wait()
    rims(rim_c, 0, RIM, 0)
    rims(rim_c, RIM + EDGE, RIM, RIM)

    @pl.loop(0, 2)
    def _(e):
        sweep(
            28 * e, range(GROUPS), range(1, GROUPS - 1),
            lambda level: 1 + 34 * e + level * (1 - 2 * e), lambda level: 2,
        )
        for k in range(2):
            @pl.when(e == k)
            def _():
                hop1(7 * k, 0)
                hop1(7 * k, 1)

    others = ids.at[pl.ds(0, n_gy - 1)]
    pltpu.make_async_copy(others, others, id_sem).wait()
    total = ids[0]
    for s in range(1, 16):
        total = total + ids[s]
    both = jnp.broadcast_to(total, (n_gy, DEPTH))
    lanes = lax.broadcasted_iota(jnp.int32, (n_gy, DEPTH), 1)
    wanted = gx * n_gy + lax.broadcasted_iota(jnp.int32, (n_gy, DEPTH), 0)
    match = (both == wanted) & (lanes < 2 * n_gy)
    least = jnp.min(jnp.where(match, lanes, 2 * n_gy - 1), axis=1, keepdims=True)
    most = jnp.max(jnp.where(match, lanes, 0), axis=1, keepdims=True)
    table_v[0] = jnp.broadcast_to(least, (n_gy, DEPTH))
    table_v[1] = jnp.broadcast_to(most, (n_gy, DEPTH))
    tab = pltpu.make_async_copy(table_v, table_s, tab_sem)
    tab.start()

    tab.wait()
    for c in ORDER:
        hop2(c)

    pltpu.make_async_copy(out, out, out_sem).wait()
    for k, sent in enumerate((rim_y, fin.at[0, 0], rim_c)):
        pltpu.make_async_copy(sent, sent, halo_send.at[k]).wait()
    for copy in smalls:
        copy.wait_send()
    pltpu.make_async_copy(others, others, id_send).wait()
    for c in range(CHUNKS):
        some = recv[c].at[pl.ds(0, 2 * n_gy - 2)]
        pltpu.make_async_copy(some, some, hop1_send.at[c]).wait()
        pltpu.make_async_copy(some, some, hop2_send.at[c]).wait()


def per_device(n_gx, n_gy, phase, solute, undercool, mobility, diffusivity, owner):
    hbm = pl.BlockSpec(memory_space=pl.ANY)
    f32 = jnp.float32
    dma = pltpu.SemaphoreType.DMA
    out = pl.pallas_call(
        functools.partial(kernel, n_gx, n_gy),
        out_shape=pltpu.VMEM((2, 2, 16, 2, EDGE, DEPTH), f32),
        in_specs=[hbm] * 6,
        out_specs=hbm,
        scratch_shapes=[
            pltpu.SMEM((1, 2), f32), pltpu.SMEM((1, 2), f32), pltpu.SMEM((1, 2), f32), pltpu.SMEM((1, 2), jnp.int32), dma((4,)),
            pltpu.VMEM((NSTEPS, 2, EDGE + 2 * RIM, 8 * GROUPS, DEPTH), f32),
            pltpu.VMEM((2, 2, 16, 2, EDGE, DEPTH), f32),
            pltpu.VMEM((2, 2, EDGE, RIM, DEPTH), f32),
            pltpu.VMEM((2, 2, 2 * RIM, RIM, DEPTH), f32),
            pltpu.VMEM((3, 4, 3, 8, DEPTH), f32),
            pltpu.VMEM((3, 4, 8, DEPTH), f32),
            pltpu.VMEM((2, 8, DEPTH), f32),
            pltpu.VMEM((1, DEPTH), jnp.int32),
            pltpu.VMEM((n_gy, 1, DEPTH), jnp.int32),
            pltpu.VMEM((2, n_gy, DEPTH), jnp.int32),
            pltpu.SMEM((2, n_gy, DEPTH), jnp.int32),
            pltpu.VMEM((CHUNKS, n_gy, 2, 2, 8, DEPTH), f32),
        ]
        + [pltpu.VMEM((2 * n_gy, 2, 8, DEPTH), f32)] * CHUNKS
        + [
            dma((4,)), dma(()), dma((2, 2, 2)), dma(()), dma((8,)), dma(()), dma(()), dma((CHUNKS,)), dma(()),
            dma((3,)), dma((8,)), dma(()), dma((CHUNKS,)), dma((CHUNKS,)),
        ],
        compiler_params=pltpu.CompilerParams(
            collective_id=0, has_side_effects=True, vmem_limit_bytes=56 << 20
        ),
    )(phase, solute, undercool, mobility, diffusivity, owner)
    shape = (1, 2, EDGE, EDGE, DEPTH)
    return out[0].reshape(shape), out[1].reshape(shape)


def solution(mesh):
    in_specs = (
        P("gx", "gy", None, None, None),
        P("gx", "gy", None, None, None),
        P("gx", "gy"),
        P("gx", "gy"),
        P("gx", "gy"),
        P("gx", "gy"),
    )
    out_specs = (P(("gx", "gy"), None, None, None, None), P(("gx", "gy"), None, None, None, None))
    return jax.shard_map(
        functools.partial(per_device, mesh.shape["gx"], mesh.shape["gy"]),
        mesh=mesh, in_specs=in_specs, out_specs=out_specs, check_vma=False,
    )
```

```python
import functools

import jax
import jax.numpy as jnp
from jax import lax
from jax.experimental import pallas as pl
from jax.experimental.pallas import tpu as pltpu
from jax.sharding import PartitionSpec as P

MESH = pl.DeviceIdType.MESH
NSTEPS = 4
RIM = 4
EDGE = 32
DEPTH = 128
GROUPS = 10
CHUNKS = 8
ORDER = (1, 2, 3, 4, 5, 6, 0, 7)

aniso_strength = 0.05
coupling = 2.0


def kernel(
    n_gx, n_gy,
    phase, solute, under, mobile, spread_in, owner,
    out,
    under_s, mobile_s, spread_s, owner_s, small_sem,
    lev, fin, rim_y, rim_c, coef, packs, own, ownid, ids, table_v, table_s, stage,
    recv0, recv1, recv2, recv3, recv4, recv5, recv6, recv7,
    in_sem, y_sem, x_sem, c_sem, coef_sem, id_sem, tab_sem, hop1_sem, out_sem,
    halo_send, coef_send, id_send, hop1_send, hop2_send,
):
    recv = (recv0, recv1, recv2, recv3, recv4, recv5, recv6, recv7)
    fields = (phase, solute)
    gx = lax.axis_index("gx")
    gy = lax.axis_index("gy")
    gx_up = lax.rem(gx + 1, n_gx)
    gx_dn = lax.rem(gx + n_gx - 1, n_gx)
    gy_up = lax.rem(gy + 1, n_gy)
    gy_dn = lax.rem(gy + n_gy - 1, n_gy)

    def remote(src, dst, send, recv_sem, device):
        return pltpu.make_async_remote_copy(
            src_ref=src, dst_ref=dst, send_sem=send, recv_sem=recv_sem,
            device_id=device, device_id_type=MESH,
        )

    loads = []
    for f in range(2):
        for b in range(2):
            loads.append(pltpu.make_async_copy(
                fields[f].at[0, b],
                lev.at[0, f, pl.ds(RIM, EDGE), pl.ds(8 + EDGE * b, EDGE), :],
                in_sem.at[2 * f + b],
            ))
    scalars = [
        pltpu.make_async_copy(src, dst, small_sem.at[k])
        for k, (src, dst) in enumerate(((under, under_s), (mobile, mobile_s), (spread_in, spread_s), (owner, owner_s)))
    ]
    for copy in scalars:
        copy.start()

    barrier = pltpu.get_barrier_semaphore()

    for d in range(1, 16):
        pl.semaphore_signal(barrier, inc=1, device_id=(gx, lax.rem(gy + d, n_gy)), device_id_type=MESH)

    for device in ((gx_up, gy), (gx_dn, gy), (gx_up, gy_up), (gx_up, gy_dn), (gx_dn, gy_up), (gx_dn, gy_dn)):
        pl.semaphore_signal(barrier, inc=1, device_id=device, device_id_type=MESH)

    for copy in loads:
        copy.start()

    for copy in scalars:
        copy.wait()
    line = lax.broadcasted_iota(jnp.int32, (8, DEPTH), 0)
    for b in range(2):
        packed = jnp.zeros((8, DEPTH), jnp.float32)
        for c, values in enumerate((under_s, mobile_s, spread_s)):
            block = jnp.full((8, DEPTH), values[0, b], jnp.float32)
            packed = jnp.where(line == c, block, packed)
            coef[1, 1 + b, c] = block
        own[b] = packed
    lane = lax.broadcasted_iota(jnp.int32, (8, DEPTH), 1)
    mine = jnp.where(lane == 2 * gy, owner_s[0, 0], 0) + jnp.where(lane == 2 * gy + 1, owner_s[0, 1], 0)
    ownid[...] = mine[:1]

    first_lane = lane == 0
    last_lane = lane == DEPTH - 1

    def advance(level, i, q):
        near = []
        for f in range(2):
            low = 8 * q
            mid = lev[level, f, i, pl.ds(low, 8), :]
            lower_x = lev[level, f, i - 1, pl.ds(low, 8), :]
            upper_x = lev[level, f, i + 1, pl.ds(low, 8), :]
            lower_y = pltpu.roll(mid, 1, 0) if q == 0 else lev[level, f, i, pl.ds(low - 1, 8), :]
            upper_y = pltpu.roll(mid, 7, 0) if q == GROUPS - 1 else lev[level, f, i, pl.ds(low + 1, 8), :]
            lower_z = jnp.where(first_lane, mid, pltpu.roll(mid, 1, 1))
            upper_z = jnp.where(last_lane, mid, pltpu.roll(mid, DEPTH - 1, 1))
            near.append((mid, lower_x, upper_x, lower_y, upper_y, lower_z, upper_z))
        zone = (i + EDGE - RIM) // EDGE
        tile = (q + 3) // 4
        under = coef[zone, tile, 0]
        mobile = coef[zone, tile, 1]
        spread = coef[zone, tile, 2]
        p, xl, xu, yl, yu, zl, zu = near[0]
        u, sxl, sxu, syl, syu, szl, szu = near[1]
        dx, dy, dz = xu - xl, yu - yl, zu - zl
        dx2, dy2, dz2 = dx * dx, dy * dy, dz * dz
        two = dx2 + dy2 + dz2
        four = dx2 * dx2 + dy2 * dy2 + dz2 * dz2
        base = two + 4.0
        top = (4.0 * aniso_strength) * four - (3.0 * aniso_strength) * (two * two)
        aniso = 1.0 + top / (base * base)
        lap = (xu + xl) + (yu + yl) + (zu + zl) - 6.0 * p
        lap_u = (sxu + sxl) + (syu + syl) + (szu + szl) - 6.0 * u
        well = 1.0 - p * p
        change = mobile * (aniso * lap + p * well - coupling * (well * well) * (under + u))
        return p + change, u + spread * lap_u + 0.5 * change

    def sweep(first, groups, last_groups, starts, pairs):
        @pl.loop(0, NSTEPS - 1)
        def _(level):
            def planes(start, count):
                for m in range(count):
                    i = start + m
                    for q in groups:
                        new_p, new_u = advance(level, i, q)
                        lev[level + 1, 0, i, pl.ds(8 * q, 8), :] = new_p
                        lev[level + 1, 1, i, pl.ds(8 * q, 8), :] = new_u

            if pairs is None:
                planes(starts(level), 4)
            else:
                pl.loop(0, pairs(level))(lambda n: planes(starts(level) + 2 * n, 2))

        @pl.loop(0, 2)
        def _(n):
            for m in range(2):
                i = first + RIM + 2 * n + m
                for q in last_groups:
                    b, g = (q - 1) // 4, (q - 1) % 4
                    new_p, new_u = advance(NSTEPS - 1, i, q)
                    fin[0, b, first // 2 + n, m, pl.ds(8 * g, 8), :] = new_p
                    fin[1, b, first // 2 + n, m, pl.ds(8 * g, 8), :] = new_u

    def sweep_inner(c, groups, last_groups):
        opening = 1 - (c + 3) // 5
        sweep(
            4 * c, groups, last_groups,
            lambda level: 4 * c + 7 - level - opening * (6 - 2 * level), lambda level: 2 + opening * (3 - level),
        )

    z, y = gy // 4, lax.rem(gy, 4)
    parity = lax.rem(z + y, 2)
    half = y // 2

    def piece(to_z, to_y, odd):
        side = to_y // 2
        g = 3 * side if odd else 1 + side
        return lax.rem(to_z, 2), pl.multiple_of(8 * g, 8), to_z // 2

    def hop1(c, odd):
        for dz in range(4):
            to_z = lax.rem(z + dz, 4)
            for m in range(2):
                to_y = 2 * lax.rem(half + m, 2) + lax.rem(to_z + odd + c, 2)
                f, row, h = piece(to_z, to_y, odd)
                src = fin.at[f, :, pl.ds(2 * c, 2), h, pl.ds(row, 8), :]
                dst = recv[c].at[pl.ds(2 * gy, 2)]

                def away():
                    remote(src, dst, hop1_send.at[c], hop1_sem.at[c], (gx, 4 * to_z + to_y)).start()

                if dz == 0 and m == 0:
                    pl.when(parity != (odd + c) % 2)(away)

                    @pl.when(parity == (odd + c) % 2)
                    def _():
                        pltpu.make_async_copy(src, dst, hop1_sem.at[c]).start()
                else:
                    away()

    my_f, my_h = lax.rem(z, 2), z // 2

    def hop2(c):
        pltpu.make_async_copy(recv[c], recv[c], hop1_sem.at[c]).wait()
        odd = lax.rem(parity + c, 2)
        row = pl.multiple_of(8 * ((1 - odd) * (1 + half) + odd * 3 * half), 8)
        dst = out.at[my_f, :, pl.ds(2 * c, 2), my_h, pl.ds(row, 8), :]
        def pick(d):
            to = lax.rem(gy + d, n_gy)
            for j in range(2):
                stage[c, to, j] = recv[c][table_s[j, to, 0]]
            return to

        @pl.loop(0, 5)
        def _(n):
            for m in range(3):
                to = pick(3 * n + m + 1)
                remote(stage.at[c, to], dst, hop2_send.at[c], out_sem, (gx, to)).start()

        to = pick(0)
        pltpu.make_async_copy(stage.at[c, to], dst, out_sem).start()

    pl.semaphore_wait(barrier, n_gy + 5)

    for f in range(2):
        remote(fields[f].at[0, 1, :, pl.ds(EDGE - RIM, RIM), :], rim_y.at[f, 0], halo_send.at[0], y_sem, (gx, gy_up)).start()
        remote(fields[f].at[0, 0, :, pl.ds(0, RIM), :], rim_y.at[f, 1], halo_send.at[0], y_sem, (gx, gy_dn)).start()
    smalls = [
        remote(own.at[1], packs.at[1, 0], coef_send.at[0], coef_sem.at[0], (gx, gy_up)),
        remote(own.at[0], packs.at[1, 3], coef_send.at[1], coef_sem.at[1], (gx, gy_dn)),
        remote(own.at[pl.ds(0, 2)], packs.at[0, pl.ds(1, 2)], coef_send.at[2], coef_sem.at[2], (gx_up, gy)),
        remote(own.at[pl.ds(0, 2)], packs.at[2, pl.ds(1, 2)], coef_send.at[3], coef_sem.at[3], (gx_dn, gy)),
        remote(own.at[1], packs.at[0, 0], coef_send.at[4], coef_sem.at[4], (gx_up, gy_up)),
        remote(own.at[0], packs.at[0, 3], coef_send.at[5], coef_sem.at[5], (gx_up, gy_dn)),
        remote(own.at[1], packs.at[2, 0], coef_send.at[6], coef_sem.at[6], (gx_dn, gy_up)),
        remote(own.at[0], packs.at[2, 3], coef_send.at[7], coef_sem.at[7], (gx_dn, gy_dn)),
    ]
    for copy in smalls[:2]:
        copy.start()
    for copy in loads:
        copy.wait()
    faces = []
    for f in range(2):
        for b in range(2):
            rows = pl.ds(8 + EDGE * b, EDGE)
            faces.append(remote(
                fields[f].at[0, b, pl.ds(EDGE - RIM, RIM)], lev.at[0, f, pl.ds(0, RIM), rows, :],
                halo_send.at[1], x_sem.at[0, f, b], (gx_up, gy)))
            faces.append(remote(
                fields[f].at[0, b, pl.ds(0, RIM)], lev.at[0, f, pl.ds(RIM + EDGE, RIM), rows, :],
                halo_send.at[1], x_sem.at[1, f, b], (gx_dn, gy)))
    corners = []
    for f in range(2):
        for xd, (planes, gx_to) in enumerate(((pl.ds(EDGE - RIM, RIM), gx_up), (pl.ds(0, RIM), gx_dn))):
            corners.append(remote(
                fields[f].at[0, 1, planes, pl.ds(EDGE - RIM, RIM), :], rim_c.at[f, 0, pl.ds(RIM * xd, RIM)],
                halo_send.at[2], c_sem, (gx_to, gy_up)))
            corners.append(remote(
                fields[f].at[0, 0, planes, pl.ds(0, RIM), :], rim_c.at[f, 1, pl.ds(RIM * xd, RIM)],
                halo_send.at[2], c_sem, (gx_to, gy_dn)))

    for copy in faces + corners + smalls[2:]:
        copy.start()
    for d in range(1, 16):
        remote(ownid, ids.at[gy], id_send, id_sem, (gx, lax.rem(gy + d, n_gy))).start()

    @pl.loop(1, 7)
    def _(c):
        sweep_inner(c, range(1, GROUPS - 1), (2, 3, 6, 7))
        for k in range(1, 7):
            pl.when(c == k)(functools.partial(hop1, k, 0))

    ids[gy] = mine[:1]

    pltpu.make_async_copy(rim_y, rim_y, y_sem).wait()
    for copy in smalls[:2]:
        copy.wait_recv()

    def unpack(zone, tiles):
        for tile in tiles:
            for c in range(3):
                coef[zone, tile, c] = jnp.broadcast_to(packs[zone, tile, pl.ds(c, 1), :], (8, DEPTH))

    unpack(1, (0, 3))

    def rims(source, lo, n, off):
        @pl.loop(0, n)
        def _(i):
            for f in range(2):
                lev[0, f, lo + i, pl.ds(RIM, RIM), :] = source[f, 0, off + i]
                lev[0, f, lo + i, pl.ds(8 + 2 * EDGE, RIM), :] = source[f, 1, off + i]

    rims(rim_y, RIM, EDGE, 0)

    @pl.loop(1, 7)
    def _(c):
        sweep_inner(c, (0, 1, GROUPS - 2, GROUPS - 1), (1, 4, 5, 8))
        for k in range(1, 7):
            pl.when(c == k)(functools.partial(hop1, k, 1))

    for copy in faces:
        copy.wait_recv()
    for copy in smalls[2:]:
        copy.wait_recv()
    unpack(0, range(4))
    unpack(2, range(4))
    pltpu.make_async_copy(rim_c, rim_c, c_sem).wait()
    rims(rim_c, 0, RIM, 0)
    rims(rim_c, RIM + EDGE, RIM, RIM)

    @pl.loop(0, 2)
    def _(e):
        sweep(
            28 * e, range(GROUPS), range(1, GROUPS - 1),
            lambda level: 1 + 34 * e + level * (1 - 2 * e), None,
        )
        for k in range(2):
            @pl.when(e == k)
            def _():
                hop1(7 * k, 0)
                hop1(7 * k, 1)

    others = ids.at[pl.ds(0, n_gy - 1)]
    pltpu.make_async_copy(others, others, id_sem).wait()
    total = ids[0]
    for s in range(1, 16):
        total = total + ids[s]
    both = jnp.broadcast_to(total, (n_gy, DEPTH))
    lanes = lax.broadcasted_iota(jnp.int32, (n_gy, DEPTH), 1)
    wanted = gx * n_gy + lax.broadcasted_iota(jnp.int32, (n_gy, DEPTH), 0)
    match = (both == wanted) & (lanes < 2 * n_gy)
    least = jnp.min(jnp.where(match, lanes, 2 * n_gy - 1), axis=1, keepdims=True)
    most = jnp.max(jnp.where(match, lanes, 0), axis=1, keepdims=True)
    table_v[0] = jnp.broadcast_to(least, (n_gy, DEPTH))
    table_v[1] = jnp.broadcast_to(most, (n_gy, DEPTH))
    tab = pltpu.make_async_copy(table_v, table_s, tab_sem)
    tab.start()

    tab.wait()
    for c in ORDER:
        hop2(c)

    pltpu.make_async_copy(out, out, out_sem).wait()
    for k, sent in enumerate((rim_y, fin.at[0, 0], rim_c)):
        pltpu.make_async_copy(sent, sent, halo_send.at[k]).wait()
    for copy in smalls:
        copy.wait_send()
    pltpu.make_async_copy(others, others, id_send).wait()
    for c in range(CHUNKS):
        some = recv[c].at[pl.ds(0, 2 * n_gy - 2)]
        pltpu.make_async_copy(some, some, hop1_send.at[c]).wait()
        pltpu.make_async_copy(some, some, hop2_send.at[c]).wait()


def per_device(n_gx, n_gy, phase, solute, undercool, mobility, diffusivity, owner):
    hbm = pl.BlockSpec(memory_space=pl.ANY)
    f32 = jnp.float32
    dma = pltpu.SemaphoreType.DMA
    out = pl.pallas_call(
        functools.partial(kernel, n_gx, n_gy),
        out_shape=pltpu.VMEM((2, 2, 16, 2, EDGE, DEPTH), f32),
        in_specs=[hbm] * 6,
        out_specs=hbm,
        scratch_shapes=[
            pltpu.SMEM((1, 2), f32), pltpu.SMEM((1, 2), f32), pltpu.SMEM((1, 2), f32), pltpu.SMEM((1, 2), jnp.int32), dma((4,)),
            pltpu.VMEM((NSTEPS, 2, EDGE + 2 * RIM, 8 * GROUPS, DEPTH), f32),
            pltpu.VMEM((2, 2, 16, 2, EDGE, DEPTH), f32),
            pltpu.VMEM((2, 2, EDGE, RIM, DEPTH), f32),
            pltpu.VMEM((2, 2, 2 * RIM, RIM, DEPTH), f32),
            pltpu.VMEM((3, 4, 3, 8, DEPTH), f32),
            pltpu.VMEM((3, 4, 8, DEPTH), f32),
            pltpu.VMEM((2, 8, DEPTH), f32),
            pltpu.VMEM((1, DEPTH), jnp.int32),
            pltpu.VMEM((n_gy, 1, DEPTH), jnp.int32),
            pltpu.VMEM((2, n_gy, DEPTH), jnp.int32),
            pltpu.SMEM((2, n_gy, DEPTH), jnp.int32),
            pltpu.VMEM((CHUNKS, n_gy, 2, 2, 8, DEPTH), f32),
        ]
        + [pltpu.VMEM((2 * n_gy, 2, 8, DEPTH), f32)] * CHUNKS
        + [
            dma((4,)), dma(()), dma((2, 2, 2)), dma(()), dma((8,)), dma(()), dma(()), dma((CHUNKS,)), dma(()),
            dma((3,)), dma((8,)), dma(()), dma((CHUNKS,)), dma((CHUNKS,)),
        ],
        compiler_params=pltpu.CompilerParams(
            collective_id=0, has_side_effects=True, vmem_limit_bytes=56 << 20
        ),
    )(phase, solute, undercool, mobility, diffusivity, owner)
    shape = (1, 2, EDGE, EDGE, DEPTH)
    return out[0].reshape(shape), out[1].reshape(shape)


def solution(mesh):
    in_specs = (
        P("gx", "gy", None, None, None),
        P("gx", "gy", None, None, None),
        P("gx", "gy"),
        P("gx", "gy"),
        P("gx", "gy"),
        P("gx", "gy"),
    )
    out_specs = (P(("gx", "gy"), None, None, None, None), P(("gx", "gy"), None, None, None, None))
    return jax.shard_map(
        functools.partial(per_device, mesh.shape["gx"], mesh.shape["gy"]),
        mesh=mesh, in_specs=in_specs, out_specs=out_specs, check_vma=False,
    )
```
